256 devices in a mesh: rep: 8 (over y, z_lo), dp: 32 (over x, z_hi, core).
Axes of the slice: x: 4, y: 4, z: 8 (z_hi: 4, z_lo: 2; z = z_hi * 2 + z_lo), core: 2. Of those that a mesh axis runs over, the one named last changes fastest.
Arguments:
- images: bfloat16 [2048, 2, 1280], P(('rep', 'dp')), may hold values from -6 to 6
- weight: bfloat16 [1280, 8192], P(None, 'dp'), may hold values from -0.3354102 to 0.3354102, as said below
Outputs:
- image_grad: float32 [2048, 2, 1280], P(('rep', 'dp'))
- weight_grad: float32 [1280, 8192], P(None, 'dp')
The draws below stay inside these ranges and needn't reach their ends.
Inputs may be any that keep to these rules, and one draw needn't show every extreme that they name: `weight`: a projection whose columns have different scales.
All inputs are finite; a program needn't handle non-finite values.
Results may differ from the reference program's by a relative error of at most 0.0021.
Values may be sent and summed in bfloat16 or wider, within the bound.
A program may use at most 64 MiB of HBM per device.

```python
import jax
import jax.numpy as jnp
from jax import lax

D_IN = 1280
EMB = 8192
IMG_DEV = 8
IMAGES = 2048
N_REP = 8
N_DP = 32


def draw_weight(key, part):
    key_values = jax.random.fold_in(key, 11)
    key_scales = jax.random.fold_in(key, 23)
    values = jnp.clip(jax.random.normal(key_values, (D_IN, EMB), jnp.float32), -4.0, 4.0)
    scales = jnp.exp(jax.random.uniform(key_scales, (1, EMB), jnp.float32, jnp.log(0.3), jnp.log(3.0)))
    return (values * scales / jnp.sqrt(jnp.float32(D_IN))).astype(jnp.bfloat16)


def levels(key, dims, shards, smallest, largest):
    level, own = 1.0, jax.random.fold_in(key, 6)
    for dim, parts in shards:
        draws = jnp.exp(jax.random.uniform(jax.random.fold_in(own, dim), (parts,), jnp.float32, smallest / len(shards), largest / len(shards)))
        level = level * jnp.repeat(draws, dims[dim] // parts).reshape([-1 if axis == dim else 1 for axis in range(len(dims))])
    return level


def scatter_about(rng, dims, scale, limit, shards=(), kind=jnp.bfloat16):
    array = scale * jax.random.normal(rng, dims, jnp.float32)
    if shards:
        array = array * levels(rng, dims, shards, -0.22, 0.18)
    return jnp.clip(array, -limit, limit).astype(kind)


def setup_inputs(seed: int = 0) -> dict:
    splits = jax.random.split(jax.random.key(seed), 3)
    images = scatter_about(splits[0], (IMAGES, 2, D_IN), 1.0, 6.0, ((0, 256),))
    weight = draw_weight(jax.random.fold_in(splits[2], 71), 0)
    return dict(images=images, weight=weight)


invariance_weight = 25.0
variance_weight = 25.0
covariance_weight = 1.0
loss_scale = 8192.0
epsilon_var = 0.0001

def group_grads(weight, rows):
    embed = jnp.einsum('mvk,ki->mvi', rows.astype(jnp.float32), weight.astype(jnp.float32))
    count = rows.shape[0]
    grad_scale = loss_scale / N_REP
    column_mean = lax.optimization_barrier(jnp.mean(embed, axis=0))
    centred = embed - column_mean
    centred_bf = centred.astype(jnp.bfloat16)
    variance = lax.optimization_barrier(jnp.sum(centred * centred, axis=0)) / (count - 1)
    spread = jnp.sqrt(variance + epsilon_var)
    coeff = grad_scale * 4.0 * covariance_weight / (EMB * (count - 1))
    block_width = EMB // N_DP

    def block_terms(index):
        begin = index * block_width
        own_cols = lax.dynamic_slice_in_dim(centred_bf, begin, block_width, 2)
        covariance = jnp.einsum('mvi,mvj->vij', own_cols.astype(jnp.float32), centred_bf.astype(jnp.float32))
        rowpos = lax.broadcasted_iota(jnp.int32, (1, block_width, EMB), 1) + begin
        colpos = lax.broadcasted_iota(jnp.int32, (1, block_width, EMB), 2)
        cov_grad = jnp.where(rowpos == colpos, 0.0, covariance / (count - 1)) * coeff
        return jnp.einsum('mvj,vij->mvi', centred_bf.astype(jnp.float32), cov_grad, precision=lax.Precision.HIGHEST)
    blocks = lax.map(block_terms, jnp.arange(N_DP, dtype=jnp.int32))
    cov_term = jnp.transpose(blocks, (1, 2, 0, 3)).reshape(count, 2, EMB)
    view_gap = embed[:, 0] - embed[:, 1]
    inv_term = jnp.stack([view_gap, -view_gap], axis=1) * (grad_scale * 2.0 * invariance_weight / (count * EMB))
    var_term = jnp.where(spread < 1.0, -grad_scale * variance_weight / (EMB * (count - 1)) / spread, 0.0) * centred
    feature_grad = (inv_term + var_term + cov_term).astype(jnp.bfloat16)
    local_grad = jnp.einsum('mvk,mvi->ki', rows.astype(jnp.float32), feature_grad.astype(jnp.float32))
    image_part = jnp.einsum('mvi,ki->mvk', feature_grad.astype(jnp.float32), weight.astype(jnp.float32))
    return (local_grad, image_part)

def reference(images, weight):
    grouped = images.reshape(N_REP, IMG_DEV * N_DP, 2, D_IN)

    def advance(running, rows):
        local_grad, image_part = group_grads(weight, rows)
        return (running + local_grad, image_part)
    weight_grad, image_parts = lax.scan(advance, jnp.zeros((D_IN, EMB), jnp.float32), grouped)
    return (image_parts.reshape(IMAGES, 2, D_IN), weight_grad)
```

```python
import jax
import jax.numpy as jnp
from jax import lax
from jax.experimental import pallas as pl
from jax.experimental.pallas import tpu as pltpu
from jax.sharding import PartitionSpec as P

MESH = pl.DeviceIdType.MESH
F32, BF16 = jnp.float32, jnp.bfloat16

N_REP, N_DP = 8, 32
M = 256
D_IN = 1280
BLOCK = 256
EMB = BLOCK * N_DP
S = 8192.0 / N_REP
EPS = 0.0001
INV = S * 2.0 * 25.0 / (M * EMB)
VAR = S * 25.0 / (EMB * (M - 1))
COV = S * 4.0 / (EMB * (M - 1))
CHUNKS = 2
WIDE = BLOCK // CHUNKS


def enc(v):
    return (v * jnp.abs(v)).astype(BF16)


def dec(b):
    t = b.astype(F32)
    s = jnp.sqrt(jnp.abs(t))
    return jnp.where(t < 0.0, -s, s)


def nt(a, b):
    return lax.dot_general(a, b, (((1,), (1,)), ((), ())), preferred_element_type=F32)


def tn(a, b):
    return lax.dot_general(a, b, (((0,), (0,)), ((), ())), preferred_element_type=F32)


def nn(a, b):
    return jnp.dot(a, b, preferred_element_type=F32)


def kernel(
    img, w, ig, wg,
    sw, X, Xo, Wo, E, Cb, base,
    T, Tx, Sz, Szr, TA,
    Ff, Fo,
    Pc, P0, Px, S32, Pz, Pzr, R, Rr,
    L32, Lc, Ly, Lz, Lzr, LA,
    send, recv,
):
    rep, dp = lax.axis_index("rep"), lax.axis_index("dp")
    y, zl = rep // 2, rep % 2
    c, chip = dp % 2, dp // 2
    x, zh = chip // 4, chip % 4

    partner = (rep, chip * 2 + (1 - c))

    def at_x(k):
        return (rep, (((x + k) % 4) * 4 + zh) * 2 + c)

    def at_z(k):
        return (rep, (x * 4 + (zh + k) % 4) * 2 + c)

    def at_y(k):
        return (((y + k) % 4) * 2 + zl, dp)

    across = (y * 2 + (1 - zl), dp)

    barrier = pltpu.get_barrier_semaphore()
    peers = [partner, across]
    for k in (1, 2, 3):
        peers += [at_x(k), at_z(k), at_y(k)]
    for peer in peers:
        pl.semaphore_signal(barrier, inc=1, device_id=peer, device_id_type=MESH)
    pl.semaphore_wait(barrier, len(peers))

    started = []

    def put(src, dst, device):
        i = len(started)
        copy = pltpu.make_async_remote_copy(
            src_ref=src, dst_ref=dst, send_sem=send.at[i], recv_sem=recv.at[i],
            device_id=device, device_id_type=MESH,
        )
        copy.start()
        started.append(copy)
        return copy

    swap = put(img.at[1 - c], sw, partner)
    wswap = put(w, Wo, partner)
    own = img[c]
    swap.wait_recv()
    other = sw[...]
    first = c == 0
    X[chip] = jnp.concatenate([jnp.where(first, own, other), jnp.where(first, other, own)], axis=0)
    zs = [put(X.at[chip], X.at[chip], at_z(k)) for k in (1, 2, 3)]
    xs = []
    for k in range(4):
        if k:
            zs[k - 1].wait_recv()
        slot = x * 4 + (zh - k + 4) % 4
        xs += [put(X.at[slot], X.at[slot], at_x(j)) for j in (1, 2, 3)]
    for copy in xs:
        copy.wait_recv()
    xswap = put(X, Xo, partner)

    rows = X[...].reshape(M, D_IN)
    wswap.wait_recv()
    for h, wr in enumerate((w, Wo)):
        e = nn(rows, wr[...])
        E[h] = e
        Cb[:, h * BLOCK:(h + 1) * BLOCK] = (e - jnp.mean(e, axis=0, keepdims=True)).astype(BF16)
    top = nt(Cb[0:128, :], Cb[...])
    low = nt(Cb[128:256, :], Cb[128:256, :])
    T[:, :, 0:256] = top.reshape(4, 32, 256)
    T[:, :, 256:384] = low.reshape(4, 32, 128)
    ts = [put(T.at[(x + k) % 4], Tx.at[k - 1], at_x(k)) for k in (1, 2, 3)]
    for copy in ts:
        copy.wait_recv()
    Sz[...] = T[x] + Tx[0] + Tx[1] + Tx[2]
    ss = [put(Sz, Szr.at[k - 1], at_z(k)) for k in (1, 2, 3)]

    xswap.wait_recv()
    orows = Xo[...].reshape(M, D_IN)
    for h, wr in enumerate((w, Wo)):
        e = E[h]
        gap = e - nn(orows, wr[...])
        centred = e - jnp.mean(e, axis=0, keepdims=True)
        spread = jnp.sqrt(jnp.sum(centred * centred, axis=0, keepdims=True) / (M - 1) + EPS)
        pull = jnp.where(spread < 1.0, -VAR / spread, 0.0)
        cb = Cb[:, h * BLOCK:(h + 1) * BLOCK].astype(F32)
        diag = jnp.sum(cb * cb, axis=0, keepdims=True) / (M - 1)
        base[h] = INV * gap + pull * centred - (COV * diag) * cb

    for copy in ss:
        copy.wait_recv()
    TA[x] = Sz[...] + Szr[0] + Szr[1] + Szr[2]
    gs = [put(TA.at[x], TA.at[x], at_x(k)) for k in (1, 2, 3)]
    for copy in gs:
        copy.wait_recv()
    top = TA[:, :, 0:256].reshape(128, 256)
    low = TA[:, :, 256:384].reshape(128, 128)
    gram = jnp.concatenate([top, jnp.concatenate([top[:, 128:256].T, low], axis=1)], axis=0)
    hi = gram.astype(BF16)
    lo = (gram - hi.astype(F32)).astype(BF16)
    for h in (1, 0):
        cb = Cb[:, h * BLOCK:(h + 1) * BLOCK]
        through = nn(hi, cb) + nn(lo, cb)
        Ff[h] = (base[h] + through * (COV / (M - 1))).astype(BF16)
        if h == 1:
            fswap = put(Ff.at[1], Fo, partner)

    ps = []
    for k in (2, 1, 3, 0):
        at = pl.ds(pl.multiple_of(((x + k) % 4) * 64, 64), 64)
        part = (nt(Ff[0, at, :], w[...]) + nt(Ff[1, at, :], Wo[...])).reshape(4, 16, D_IN)
        if k:
            Pc[k - 1] = enc(part)
            ps.append(put(Pc.at[k - 1], Px.at[k - 1], at_x(k)))
        else:
            P0[...] = part

    fswap.wait_recv()
    for j in range(5):
        cols = pl.ds(j * 256, 256)
        L32[cols, :] = tn(X[:, :, cols].reshape(M, 256), Ff[0]) + tn(Xo[:, :, cols].reshape(M, 256), Fo[...])
    ys = []
    for h in range(CHUNKS):
        lanes = pl.ds(h * WIDE, WIDE)
        for k in (2, 1, 3):
            at = pl.ds(pl.multiple_of(((y + k) % 4) * 320, 320), 320)
            Lc[h, k - 1] = enc(L32[at, lanes])
            ys.append(put(Lc.at[h, k - 1], Ly.at[h, k - 1], at_y(k)))

    for copy in ps:
        copy.wait_recv()
    for j in range(4):
        s = P0[j] + dec(Px[0, j]) + dec(Px[1, j]) + dec(Px[2, j])
        S32[j] = s
        Pz[j] = enc(s)
    pz = [put(Pz.at[(zh + k) % 4], Pzr.at[k - 1], at_z(k)) for k in (2, 1, 3)]

    mine = pl.ds(pl.multiple_of(y * 320, 320), 320)
    zz = []
    for h in range(CHUNKS):
        for copy in ys[3 * h:3 * h + 3]:
            copy.wait_recv()
        lanes = pl.ds(h * WIDE, WIDE)
        s = L32[mine, lanes] + dec(Ly[h, 0]) + dec(Ly[h, 1]) + dec(Ly[h, 2])
        Lz[h] = enc(s)
        zz.append(put(Lz.at[h], Lzr.at[h], across))

    for copy in pz:
        copy.wait_recv()
    r = S32[zh] + dec(Pzr[0]) + dec(Pzr[1]) + dec(Pzr[2])
    R[...] = r.reshape(2, 8, D_IN)
    rswap = put(R.at[1 - c], Rr, partner)

    ls = []
    for h in range(CHUNKS):
        zz[h].wait_recv()
        LA[h, y] = enc(dec(Lz[h]) + dec(Lzr[h]))
        ls += [put(LA.at[h, y], LA.at[h, y], at_y(k)) for k in (2, 1, 3)]

    rswap.wait_recv()
    ig[c] = R[c]
    ig[1 - c] = Rr[...]

    for h in range(CHUNKS):
        for copy in ls[3 * h:3 * h + 3]:
            copy.wait_recv()
        for j in range(4):
            wg[j * 320:(j + 1) * 320, h * WIDE:(h + 1) * WIDE] = dec(LA[h, j])
    for copy in started:
        copy.wait_send()


def shards(images, weight):
    V = pltpu.VMEM
    ig, wg = pl.pallas_call(
        kernel,
        out_shape=(
            jax.ShapeDtypeStruct((2, 8, D_IN), F32),
            jax.ShapeDtypeStruct((D_IN, BLOCK), F32),
        ),
        in_specs=[pl.BlockSpec(memory_space=V)] * 2,
        out_specs=[pl.BlockSpec(memory_space=V)] * 2,
        scratch_shapes=[
            V((8, D_IN), BF16),
            V((16, 16, D_IN), BF16),
            V((16, 16, D_IN), BF16),
            V((D_IN, BLOCK), BF16),
            V((2, M, BLOCK), F32),
            V((M, 2 * BLOCK), BF16),
            V((2, M, BLOCK), F32),
            V((4, 32, 384), F32),
            V((3, 32, 384), F32),
            V((32, 384), F32),
            V((3, 32, 384), F32),
            V((4, 32, 384), F32),
            V((2, M, BLOCK), BF16),
            V((M, BLOCK), BF16),
            V((3, 4, 16, D_IN), BF16),
            V((4, 16, D_IN), F32),
            V((3, 4, 16, D_IN), BF16),
            V((4, 16, D_IN), F32),
            V((4, 16, D_IN), BF16),
            V((3, 16, D_IN), BF16),
            V((2, 8, D_IN), F32),
            V((8, D_IN), F32),
            V((D_IN, BLOCK), F32),
            V((CHUNKS, 3, 320, WIDE), BF16),
            V((CHUNKS, 3, 320, WIDE), BF16),
            V((CHUNKS, 320, WIDE), BF16),
            V((CHUNKS, 320, WIDE), BF16),
            V((CHUNKS, 4, 320, WIDE), BF16),
            pltpu.SemaphoreType.DMA((64,)),
            pltpu.SemaphoreType.DMA((64,)),
        ],
        compiler_params=pltpu.CompilerParams(
            collective_id=0, has_side_effects=True, vmem_limit_bytes=60 * 2**20
        ),
    )(images.transpose(1, 0, 2), weight)
    return ig.transpose(1, 0, 2), wg


def solution(mesh):
    return jax.shard_map(
        shards,
        mesh=mesh,
        in_specs=(P(("rep", "dp"), None, None), P(None, "dp")),
        out_specs=(P(("rep", "dp"), None, None), P(None, "dp")),
        check_vma=False,
    )
```

```python
import jax
import jax.numpy as jnp
from jax import lax
from jax.experimental import pallas as pl
from jax.experimental.pallas import tpu as pltpu
from jax.sharding import PartitionSpec as P

MESH = pl.DeviceIdType.MESH
F32, BF16 = jnp.float32, jnp.bfloat16

N_REP, N_DP = 8, 32
M = 256
D_IN = 1280
BLOCK = 256
EMB = BLOCK * N_DP
S = 8192.0 / N_REP
EPS = 0.0001
INV = S * 2.0 * 25.0 / (M * EMB)
VAR = S * 25.0 / (EMB * (M - 1))
COV = S * 4.0 / (EMB * (M - 1))
CHUNKS = 2
WIDE = BLOCK // CHUNKS
CUT = 1024
REST = D_IN - CUT
GRAM_UNIT = 2.0**-10


def root(t):
    return jnp.sqrt(jnp.abs(t))


def enc(v):
    return (v * jnp.abs(v)).astype(BF16)


def dec(b):
    t = b.astype(F32)
    s = root(t)
    return jnp.where(t < 0.0, -s, s)


def enc4(g):
    v = g * GRAM_UNIT
    return ((v * jnp.abs(v)) * (v * v)).astype(BF16)


def dec4(b):
    t = b.astype(F32)
    s = root(root(t)) * (1.0 / GRAM_UNIT)
    return jnp.where(t < 0.0, -s, s)


def nt(a, b):
    return lax.dot_general(a, b, (((1,), (1,)), ((), ())), preferred_element_type=F32)


def tn(a, b):
    return lax.dot_general(a, b, (((0,), (0,)), ((), ())), preferred_element_type=F32)


def nn(a, b):
    return jnp.dot(a, b, preferred_element_type=F32)


def kernel(
    img, w, ig, lg,
    I2, X, Xo, Wo, WT, E, Cb, base,
    T, Tc, Tx, Sz, Sc, Szr, TA,
    Ff, Fo,
    Pc, P0, Px, S32, Pz, Pzr,
    B32, Bc, Bz, B2, Bx, Bxr, R, Rr,
    L32, Lc, Ly, Lz, Lzr, La,
    send, recv, local,
):
    rep, dp = lax.axis_index("rep"), lax.axis_index("dp")
    y, zl = rep // 2, rep % 2
    c, chip = dp % 2, dp // 2
    x, zh = chip // 4, chip % 4
    o = 1 - c

    partner = (rep, chip * 2 + o)

    def at_x(k, core):
        return (rep, (((x + k) % 4) * 4 + zh) * 2 + core)

    def at_z(k, core):
        return (rep, (x * 4 + (zh + k) % 4) * 2 + core)

    def at_y(k):
        return (((y + k) % 4) * 2 + zl, dp)

    across = (y * 2 + (1 - zl), dp)

    barrier = pltpu.get_barrier_semaphore()
    peers = [partner, across]
    for k in (1, 2, 3):
        peers += [at_x(k, c), at_z(k, c), at_x(k, o), at_z(k, o), at_y(k)]
    for peer in peers:
        pl.semaphore_signal(barrier, inc=1, device_id=peer, device_id_type=MESH)
    both = img[...].astype(F32)
    I2[0] = both[:, 0, :].astype(BF16)
    I2[1] = both[:, 1, :].astype(BF16)
    pl.semaphore_wait(barrier, len(peers))

    started = []

    def put(src, dst, device):
        i = len(started)
        copy = pltpu.make_async_remote_copy(
            src_ref=src, dst_ref=dst, send_sem=send.at[i], recv_sem=recv.at[i],
            device_id=device, device_id_type=MESH,
        )
        copy.start()
        started.append(copy)
        return copy

    at = pl.ds(pl.multiple_of(c * 8, 8), 8)
    A, B = pl.ds(0, CUT), pl.ds(CUT, REST)
    az, bx = [], []
    for k in (2, 1, 3):
        for core in (c, o):
            az.append(put(I2.at[core, :, A], X.at[chip, at, A], at_z(k, core)))
            bx.append(put(I2.at[core, :, B], X.at[chip, at, B], at_x(k, core)))
    mate = put(I2.at[o], X.at[chip, at], partner)
    keep = pltpu.make_async_copy(I2.at[c], X.at[chip, at], local.at[0])
    keep.start()
    wswap = put(w, Wo, partner)
    keep.wait()
    mate.wait_recv()
    forwards = []
    for k in (0, 1, 3, 2):
        if k:
            j = (2, 1, 3).index(k) * 2
            az[j].wait_recv()
            az[j + 1].wait_recv()
        slot = x * 4 + (zh - k + 4) % 4
        forwards += [put(X.at[slot, :, A], X.at[slot, :, A], at_x(j, c)) for j in (2, 1, 3)]
        if k:
            j = (2, 1, 3).index(k) * 2
            bx[j].wait_recv()
            bx[j + 1].wait_recv()
        slot = ((x - k + 4) % 4) * 4 + zh
        forwards += [put(X.at[slot, :, B], X.at[slot, :, B], at_z(j, c)) for j in (2, 1, 3)]
    wswap.wait_recv()
    WT[0] = w[...].T
    WT[1] = Wo[...].T
    for copy in forwards:
        copy.wait_recv()
    xswap = put(X, Xo, partner)

    rows = X[...].reshape(M, D_IN)
    for h, wr in enumerate((w, Wo)):
        e = nn(rows, wr[...])
        E[h] = e
        Cb[:, h * BLOCK:(h + 1) * BLOCK] = (e - jnp.mean(e, axis=0, keepdims=True)).astype(BF16)
    top = nt(Cb[0:128, :], Cb[...])
    low = nt(Cb[128:256, :], Cb[128:256, :])
    T[:, :, 0:256] = top.reshape(4, 32, 256)
    T[:, :, 256:384] = low.reshape(4, 32, 128)
    Tc[:, :, 0:256] = enc4(top).reshape(4, 32, 256)
    Tc[:, :, 256:384] = enc4(low).reshape(4, 32, 128)
    ts = [put(Tc.at[(x + k) % 4], Tx.at[k - 1], at_x(k, c)) for k in (2, 1, 3)]
    for copy in ts:
        copy.wait_recv()
    s = T[x] + dec4(Tx[0]) + dec4(Tx[1]) + dec4(Tx[2])
    Sz[...] = s
    Sc[...] = enc4(s)
    ss = [put(Sc, Szr.at[k - 1], at_z(k, c)) for k in (2, 1, 3)]

    xswap.wait_recv()
    orows = Xo[...].reshape(M, D_IN)
    for h, wr in enumerate((w, Wo)):
        e = E[h]
        gap = e - nn(orows, wr[...])
        centred = e - jnp.mean(e, axis=0, keepdims=True)
        spread = jnp.sqrt(jnp.sum(centred * centred, axis=0, keepdims=True) / (M - 1) + EPS)
        pull = jnp.where(spread < 1.0, -VAR / spread, 0.0)
        cb = Cb[:, h * BLOCK:(h + 1) * BLOCK].astype(F32)
        diag = jnp.sum(cb * cb, axis=0, keepdims=True) / (M - 1)
        base[h] = INV * gap + pull * centred - (COV * diag) * cb

    for copy in ss:
        copy.wait_recv()
    TA[x] = enc4(Sz[...] + dec4(Szr[0]) + dec4(Szr[1]) + dec4(Szr[2]))
    gs = [put(TA.at[x], TA.at[x], at_x(k, c)) for k in (2, 1, 3)]
    for copy in gs:
        copy.wait_recv()
    top = dec4(TA[:, :, 0:256].reshape(128, 256))
    low = dec4(TA[:, :, 256:384].reshape(128, 128))
    gram = jnp.concatenate([top, jnp.concatenate([top[:, 128:256].T, low], axis=1)], axis=0)
    hi = gram.astype(BF16)
    lo = (gram - hi.astype(F32)).astype(BF16)
    for h in (1, 0):
        cb = Cb[:, h * BLOCK:(h + 1) * BLOCK]
        through = nn(hi, cb) + nn(lo, cb)
        Ff[h] = (base[h] + through * (COV / (M - 1))).astype(BF16)
        if h == 1:
            fswap = put(Ff.at[1], Fo, partner)

    ps = []
    for k in (2, 1, 3, 0):
        at = pl.ds(pl.multiple_of(((x + k) % 4) * 64, 64), 64)
        part = (nn(Ff[0, at, :], WT[0, :, 0:CUT]) + nn(Ff[1, at, :], WT[1, :, 0:CUT])).reshape(4, 16, CUT)
        if k:
            Pc[k - 1] = enc(part)
            ps.append(put(Pc.at[k - 1], Px.at[k - 1], at_x(k, c)))
        else:
            P0[...] = part
    part = (nn(Ff[0], WT[0, :, CUT:D_IN]) + nn(Ff[1], WT[1, :, CUT:D_IN])).reshape(4, 4, 16, REST)
    for j in range(4):
        B32[j] = part[:, j]
        Bc[j] = enc(part[:, j])
    bz = [put(Bc.at[(zh + k) % 4], Bz.at[k - 1], at_z(k, c)) for k in (2, 1, 3)]

    fswap.wait_recv()
    for j in range(5):
        cols = pl.ds(j * 256, 256)
        L32[cols, :] = tn(X[:, :, cols].reshape(M, 256), Ff[0]) + tn(Xo[:, :, cols].reshape(M, 256), Fo[...])
    ys = []
    for h in range(CHUNKS):
        lanes = pl.ds(h * WIDE, WIDE)
        for k in (2, 1, 3):
            at = pl.ds(pl.multiple_of(((y + k) % 4) * 320, 320), 320)
            Lc[h, k - 1] = enc(L32[at, lanes])
            ys.append(put(Lc.at[h, k - 1], Ly.at[h, k - 1], at_y(k)))

    for copy in bz:
        copy.wait_recv()
    for j in range(4):
        s = B32[zh, j] + dec(Bz[0, j]) + dec(Bz[1, j]) + dec(Bz[2, j])
        B2[j] = s
        Bx[j] = enc(s)
    bs = [put(Bx.at[(x + k) % 4], Bxr.at[k - 1], at_x(k, c)) for k in (2, 1, 3)]

    for copy in ps:
        copy.wait_recv()
    for j in range(4):
        s = P0[j] + dec(Px[0, j]) + dec(Px[1, j]) + dec(Px[2, j])
        S32[j] = s
        Pz[j] = enc(s)
    pz = [put(Pz.at[(zh + k) % 4], Pzr.at[k - 1], at_z(k, c)) for k in (2, 1, 3)]

    mine = pl.ds(pl.multiple_of(y * 320, 320), 320)
    zz = []
    for h in range(CHUNKS):
        for copy in ys[3 * h:3 * h + 3]:
            copy.wait_recv()
        lanes = pl.ds(h * WIDE, WIDE)
        s = L32[mine, lanes] + dec(Ly[h, 0]) + dec(Ly[h, 1]) + dec(Ly[h, 2])
        Lz[h] = enc(s)
        zz.append(put(Lz.at[h], Lzr.at[h], across))

    ls, kept = [], []
    for h in range(CHUNKS):
        zz[h].wait_recv()
        La[h] = enc(dec(Lz[h]) + dec(Lzr[h]))
        there = lg.at[mine, pl.ds(h * WIDE, WIDE)]
        ls += [put(La.at[h], there, at_y(k)) for k in (2, 1, 3)]
        kept.append(pltpu.make_async_copy(La.at[h], there, local.at[1 + h]))
        kept[-1].start()

    for copy in pz + bs:
        copy.wait_recv()
    r = S32[zh] + dec(Pzr[0]) + dec(Pzr[1]) + dec(Pzr[2])
    R[:, :, 0:CUT] = r.reshape(2, 8, CUT)
    r = B2[x] + dec(Bxr[0]) + dec(Bxr[1]) + dec(Bxr[2])
    R[:, :, CUT:D_IN] = r.reshape(2, 8, REST)
    rswap = put(R.at[o], Rr, partner)
    rswap.wait_recv()
    own, other = R[c], Rr[...]
    first = c == 0
    ig[:, 0, :] = jnp.where(first, own, other)
    ig[:, 1, :] = jnp.where(first, other, own)

    for copy in ls:
        copy.wait_recv()
    for copy in kept:
        copy.wait()
    for copy in started:
        copy.wait_send()


def shards(images, weight):
    V = pltpu.VMEM
    ig, lg = pl.pallas_call(
        kernel,
        out_shape=(
            jax.ShapeDtypeStruct((8, 2, D_IN), F32),
            jax.ShapeDtypeStruct((D_IN, BLOCK), BF16),
        ),
        in_specs=[pl.BlockSpec(memory_space=V)] * 2,
        out_specs=[pl.BlockSpec(memory_space=V), pl.BlockSpec(memory_space=LGSPACE)],
        scratch_shapes=[
            V((2, 8, D_IN), BF16),
            V((16, 16, D_IN), BF16),
            V((16, 16, D_IN), BF16),
            V((D_IN, BLOCK), BF16),
            V((2, BLOCK, D_IN), BF16),
            V((2, M, BLOCK), F32),
            V((M, 2 * BLOCK), BF16),
            V((2, M, BLOCK), F32),
            V((4, 32, 384), F32),
            V((4, 32, 384), BF16),
            V((3, 32, 384), BF16),
            V((32, 384), F32),
            V((32, 384), BF16),
            V((3, 32, 384), BF16),
            V((4, 32, 384), BF16),
            V((2, M, BLOCK), BF16),
            V((M, BLOCK), BF16),
            V((3, 4, 16, CUT), BF16),
            V((4, 16, CUT), F32),
            V((3, 4, 16, CUT), BF16),
            V((4, 16, CUT), F32),
            V((4, 16, CUT), BF16),
            V((3, 16, CUT), BF16),
            V((4, 4, 16, REST), F32),
            V((4, 4, 16, REST), BF16),
            V((3, 4, 16, REST), BF16),
            V((4, 16, REST), F32),
            V((4, 16, REST), BF16),
            V((3, 16, REST), BF16),
            V((2, 8, D_IN), F32),
            V((8, D_IN), F32),
            V((D_IN, BLOCK), F32),
            V((CHUNKS, 3, 320, WIDE), BF16),
            V((CHUNKS, 3, 320, WIDE), BF16),
            V((CHUNKS, 320, WIDE), BF16),
            V((CHUNKS, 320, WIDE), BF16),
            V((CHUNKS, 320, WIDE), BF16),
            pltpu.SemaphoreType.DMA((96,)),
            pltpu.SemaphoreType.DMA((96,)),
            pltpu.SemaphoreType.DMA((4,)),
        ],
        compiler_params=pltpu.CompilerParams(
            collective_id=0, has_side_effects=True, vmem_limit_bytes=VLIM
        ),
    )(images, weight)
    return ig, dec(lg)


LGSPACE = pl.ANY
VLIM = 24 * 2**20


def solution(mesh):
    return jax.shard_map(
        shards,
        mesh=mesh,
        in_specs=(P(("rep", "dp"), None, None), P(None, "dp")),
        out_specs=(P(("rep", "dp"), None, None), P(None, "dp")),
        check_vma=False,
    )
```

```python
import jax
import jax.numpy as jnp
from jax import lax
from jax.experimental import pallas as pl
from jax.experimental.pallas import tpu as pltpu
from jax.sharding import PartitionSpec as P

MESH = pl.DeviceIdType.MESH
F32, BF16 = jnp.float32, jnp.bfloat16

N_REP, N_DP = 8, 32
M = 256
D_IN = 1280
BLOCK = 256
EMB = BLOCK * N_DP
S = 8192.0 / N_REP
EPS = 0.0001
INV = S * 2.0 * 25.0 / (M * EMB)
VAR = S * 25.0 / (EMB * (M - 1))
COV = S * 4.0 / (EMB * (M - 1))
CHUNKS = 4
ROWS = D_IN // 4 // CHUNKS
CUT = 1024
REST = D_IN - CUT
GRAM_UNIT = 2.0**-10


def root(t):
    return jnp.sqrt(jnp.abs(t))


def enc(v):
    return (v * jnp.abs(v)).astype(BF16)


def dec(b):
    t = b.astype(F32)
    s = root(t)
    return jnp.where(t < 0.0, -s, s)


def enc4(g):
    v = g * GRAM_UNIT
    return ((v * jnp.abs(v)) * (v * v)).astype(BF16)


def dec4(b):
    t = b.astype(F32)
    s = root(root(t)) * (1.0 / GRAM_UNIT)
    return jnp.where(t < 0.0, -s, s)


def nt(a, b):
    return lax.dot_general(a, b, (((1,), (1,)), ((), ())), preferred_element_type=F32)


def tn(a, b):
    return lax.dot_general(a, b, (((0,), (0,)), ((), ())), preferred_element_type=F32)


def nn(a, b):
    return jnp.dot(a, b, preferred_element_type=F32)


class Group:
    def __init__(self, sem):
        self.sem, self.kib = sem, 0


def kernel(
    img, w_hbm, ig, lg,
    Iv, w, I2, X, Xo, Wo, WT, E, Cb, base,
    T, Tc, Tx, Sz, Sc, Szr, TA, Dg, Dx, Ds, Dz,
    Ff, Fo,
    Pc, P0, Px, S32, Pz, Pzr,
    B32, Bc, Bz, B2, Bx, Bxr, R, Rr,
    L32, Lo, Ld, Lc, Ro, Rd, Rc, Lz, Lzr, La,
    span, send, recv, local,
):
    rep, dp = lax.axis_index("rep"), lax.axis_index("dp")
    y, zl = rep // 2, rep % 2
    c, chip = dp % 2, dp // 2
    x, zh = chip // 4, chip % 4
    o = 1 - c

    partner = (rep, chip * 2 + o)

    def at_x(k, core):
        return (rep, (((x + k) % 4) * 4 + zh) * 2 + core)

    def at_z(k, core):
        return (rep, (x * 4 + (zh + k) % 4) * 2 + core)

    def at_y(k):
        return (((y + k) % 4) * 2 + zl, dp)

    across = (y * 2 + (1 - zl), dp)

    fetch = pltpu.make_async_copy(img, Iv, local.at[0])
    fetch.start()
    wfetch = pltpu.make_async_copy(w_hbm, w, local.at[1])
    wfetch.start()
    barrier = pltpu.get_barrier_semaphore()
    peers = [partner, across]
    for k in (1, 2, 3):
        peers += [at_x(k, c), at_z(k, c), at_x(k, o), at_z(k, o), at_y(k)]
    for peer in peers:
        pl.semaphore_signal(barrier, inc=1, device_id=peer, device_id_type=MESH)
    fetch.wait()
    both = Iv[...].astype(F32)
    I2[0] = both[:, 0, :].astype(BF16)
    I2[1] = both[:, 1, :].astype(BF16)
    pl.semaphore_wait(barrier, len(peers))

    sent = Group(send)
    groups = []

    def group():
        groups.append(Group(recv.at[len(groups)]))
        return groups[-1]

    def put(src, dst, device, at=None):
        at = at or group()
        copy = pltpu.make_async_remote_copy(
            src_ref=src, dst_ref=dst, send_sem=sent.sem, recv_sem=at.sem,
            device_id=device, device_id_type=MESH,
        )
        copy.start()
        size = 1
        for n in src.shape:
            size *= n
        kib = size * jnp.dtype(src.dtype).itemsize // 1024
        at.kib += kib
        sent.kib += kib
        return at

    def wait(at):
        part = span.at[pl.ds(0, at.kib * 2)]
        pltpu.make_async_copy(part, part, at.sem).wait()

    at = pl.ds(pl.multiple_of(c * 8, 8), 8)
    A, B = pl.ds(0, CUT), pl.ds(CUT, REST)
    az, bx = {}, {}
    for k in (1, 3, 2):
        az[k], bx[k] = group(), group()
        for core in (c, o):
            put(I2.at[core, :, A], X.at[chip, at, A], at_z(k, core), az[k])
            put(I2.at[core, :, B], X.at[chip, at, B], at_x(k, core), bx[k])
    mate = put(I2.at[o], X.at[chip, at], partner)
    keep = pltpu.make_async_copy(I2.at[c], X.at[chip, at], local.at[0])
    keep.start()
    wswap = put(w_hbm, Wo, partner)
    keep.wait()
    wait(mate)
    forwards = group()
    for k in (0, 1, 3, 2):
        if k:
            wait(az[k])
        slot = x * 4 + (zh - k + 4) % 4
        for j in (2, 1, 3):
            put(X.at[slot, :, A], X.at[slot, :, A], at_x(j, c), forwards)
        if k:
            wait(bx[k])
        slot = ((x - k + 4) % 4) * 4 + zh
        for j in (2, 1, 3):
            put(X.at[slot, :, B], X.at[slot, :, B], at_z(j, c), forwards)
    wait(wswap)
    wfetch.wait()
    WT[0] = w[...].T
    WT[1] = Wo[...].T
    wait(forwards)
    xswap = put(X, Xo, partner)

    rows = X[...].reshape(M, D_IN)
    for h, wr in enumerate((w, Wo)):
        e = nn(rows, wr[...])
        E[h] = e
        Cb[:, h * BLOCK:(h + 1) * BLOCK] = (e - jnp.mean(e, axis=0, keepdims=True)).astype(BF16)
    ri = lax.broadcasted_iota(jnp.int32, (128, 128), 0)
    ci = lax.broadcasted_iota(jnp.int32, (128, 128), 1)
    top = nt(Cb[0:128, :], Cb[...])
    low = nt(Cb[128:256, :], Cb[128:256, :])
    mixed = jnp.where(ri <= ci, top[:, 0:128], low)
    T[:, :, 0:128] = mixed.reshape(4, 32, 128)
    T[:, :, 128:256] = top[:, 128:256].reshape(4, 32, 128)
    Tc[...] = enc4(T[...])
    diags = [jnp.sum(jnp.where(ri == ci, g, 0.0), axis=0, keepdims=True) for g in (top[:, 0:128], low)]
    Dg[...] = jnp.where(lax.broadcasted_iota(jnp.int32, (8, 128), 0) == 0, diags[0], diags[1])
    ts = group()
    for k in (2, 1, 3):
        put(Tc.at[(x + k) % 4], Tx.at[k - 1], at_x(k, c), ts)
        put(Dg, Dx.at[k - 1], at_x(k, c), ts)
    wait(ts)
    s = T[x] + dec4(Tx[0]) + dec4(Tx[1]) + dec4(Tx[2])
    Sz[...] = s
    Sc[...] = enc4(s)
    Ds[...] = Dg[...] + Dx[0] + Dx[1] + Dx[2]
    ss = group()
    for k in (2, 1, 3):
        put(Sc, Szr.at[k - 1], at_z(k, c), ss)
        put(Ds, Dz.at[k - 1], at_z(k, c), ss)

    wait(xswap)
    orows = Xo[...].reshape(M, D_IN)
    for h, wr in enumerate((w, Wo)):
        e = E[h]
        gap = e - nn(orows, wr[...])
        centred = e - jnp.mean(e, axis=0, keepdims=True)
        spread = jnp.sqrt(jnp.sum(centred * centred, axis=0, keepdims=True) / (M - 1) + EPS)
        pull = jnp.where(spread < 1.0, -VAR / spread, 0.0)
        cb = Cb[:, h * BLOCK:(h + 1) * BLOCK].astype(F32)
        diag = jnp.sum(cb * cb, axis=0, keepdims=True) / (M - 1)
        base[h] = INV * gap + pull * centred - (COV * diag) * cb

    wait(ss)
    TA[x] = enc4(Sz[...] + dec4(Szr[0]) + dec4(Szr[1]) + dec4(Szr[2]))
    gs = group()
    for k in (2, 1, 3):
        put(TA.at[x], TA.at[x], at_x(k, c), gs)
    diags = Ds[...] + Dz[0] + Dz[1] + Dz[2]
    wait(gs)
    mixed = dec4(TA[:, :, 0:128].reshape(128, 128))
    side = dec4(TA[:, :, 128:256].reshape(128, 128))
    flip = mixed.T
    ga = jnp.where(ri == ci, diags[0:1], jnp.where(ri < ci, mixed, flip))
    gd = jnp.where(ri == ci, diags[1:2], jnp.where(ri > ci, mixed, flip))
    gram = jnp.concatenate(
        [jnp.concatenate([ga, side], axis=1), jnp.concatenate([side.T, gd], axis=1)], axis=0
    )
    hi = gram.astype(BF16)
    lo = (gram - hi.astype(F32)).astype(BF16)
    for h in (1, 0):
        cb = Cb[:, h * BLOCK:(h + 1) * BLOCK]
        through = nn(hi, cb) + nn(lo, cb)
        Ff[h] = (base[h] + through * (COV / (M - 1))).astype(BF16)
        if h == 1:
            fswap = put(Ff.at[1], Fo, partner)

    def part_a(k):
        at = pl.ds(pl.multiple_of(((x + k) % 4) * 64, 64), 64)
        part = nn(Ff[0, at, :], WT[0, :, 0:CUT]) + nn(Ff[1, at, :], WT[1, :, 0:CUT])
        return part.reshape(4, 16, CUT)

    part = (nn(Ff[0], WT[0, :, CUT:D_IN]) + nn(Ff[1], WT[1, :, CUT:D_IN])).reshape(4, 4, 16, REST)
    for j in range(4):
        B32[j] = part[:, j]
        Bc[j] = enc(part[:, j])
    bz = group()
    for k in (2, 1, 3):
        put(Bc.at[(zh + k) % 4], Bz.at[k - 1], at_z(k, c), bz)
    ps = group()
    for k in (2, 1, 3):
        Pc[k - 1] = enc(part_a(k))
        put(Pc.at[k - 1], Px.at[k - 1], at_x(k, c), ps)

    wait(fswap)
    for j in range(5):
        cols = pl.ds(j * 256, 256)
        L32[cols, :] = tn(X[:, :, cols].reshape(M, 256), Ff[0]) + tn(Xo[:, :, cols].reshape(M, 256), Fo[...])

    def rows_of(k, q):
        return pl.ds(pl.multiple_of(((y + k) % 4) * 320 + q * ROWS, ROWS), ROWS)

    sides = (pl.ds(0, 128), pl.ds(128, 128))
    ways = (1, 3)
    opp, direct, joint = {}, {}, {}
    for q in range(CHUNKS):
        opp[q], direct[q] = group(), group()
        for i in range(2):
            Lo[q, i] = enc(L32[rows_of(2, q), sides[i]])
            put(Lo.at[q, i], Ro.at[q, i], at_y(ways[i]), opp[q])

    def send_direct(q):
        for i in range(2):
            Ld[q, i] = enc(L32[rows_of(ways[i], q), sides[1 - i]])
            put(Ld.at[q, i], Rd.at[q, 1 - i], at_y(ways[i]), direct[q])

    send_direct(0)
    P0[...] = part_a(0)
    for q in range(CHUNKS):
        wait(opp[q])
        for i in range(2):
            Lc[q, i] = enc(L32[rows_of(ways[i], q), sides[i]] + dec(Ro[q, i]))
            put(Lc.at[q, i], Rc.at[q, i], at_y(ways[i]), direct[q])
        if q + 1 < CHUNKS:
            send_direct(q + 1)
    zz = []
    for q in range(CHUNKS):
        wait(direct[q])
        for i in range(2):
            Lz[q, i] = enc(L32[rows_of(0, q), sides[i]] + dec(Rd[q, i]) + dec(Rc[q, i]))
        zz.append(put(Lz.at[q], Lzr.at[q], across))

    wait(bz)
    for j in range(4):
        s = B32[zh, j] + dec(Bz[0, j]) + dec(Bz[1, j]) + dec(Bz[2, j])
        B2[j] = s
        Bx[j] = enc(s)
    bs = group()
    for k in (2, 1, 3):
        put(Bx.at[(x + k) % 4], Bxr.at[k - 1], at_x(k, c), bs)

    wait(ps)
    for j in range(4):
        s = P0[j] + dec(Px[0, j]) + dec(Px[1, j]) + dec(Px[2, j])
        S32[j] = s
        Pz[j] = enc(s)
    pz = group()
    for k in (2, 1, 3):
        put(Pz.at[(zh + k) % 4], Pzr.at[k - 1], at_z(k, c), pz)

    ls, kept = {}, []
    last = group()
    for q in range(CHUNKS):
        wait(zz[q])
        for i in range(2):
            La[q, :, sides[i]] = enc(dec(Lz[q, i]) + dec(Lzr[q, i]))
        here = lg.at[rows_of(0, q)]
        ls[q] = group()
        for way in ways:
            put(La.at[q], here, at_y(way), ls[q])
        kept.append(pltpu.make_async_copy(La.at[q], here, local.at[q]))
        kept[-1].start()

    for q in range(CHUNKS):
        wait(ls[q])
        for i in range(2):
            there = lg.at[rows_of(4 - ways[i], q), sides[i]]
            put(there, there, at_y(ways[i]), last)

    wait(pz)
    r = S32[zh] + dec(Pzr[0]) + dec(Pzr[1]) + dec(Pzr[2])
    R[:, :, 0:CUT] = r.reshape(2, 8, CUT)
    wait(bs)
    r = B2[x] + dec(Bxr[0]) + dec(Bxr[1]) + dec(Bxr[2])
    R[:, :, CUT:D_IN] = r.reshape(2, 8, REST)
    rswap = put(R.at[o], Rr, partner)
    wait(rswap)
    own, other = R[c], Rr[...]
    first = c == 0
    ig[:, 0, :] = jnp.where(first, own, other)
    ig[:, 1, :] = jnp.where(first, other, own)

    wait(last)
    for copy in kept:
        copy.wait()
    wait(sent)


def finish(ig, lg, image_grad, weight_grad, full, sem):
    copies = [pltpu.make_async_copy(ig, image_grad, sem.at[0])]
    copies[0].start()
    for j in range(5):
        at = pl.ds(j * 256, 256)
        full[at] = dec(lg[at])
        copies.append(pltpu.make_async_copy(full.at[at], weight_grad.at[at], sem.at[1 + j]))
        copies[-1].start()
    for copy in copies:
        copy.wait()


def shards(images, weight):
    V = pltpu.VMEM
    ig, lg = pl.pallas_call(
        kernel,
        out_shape=(
            jax.ShapeDtypeStruct((8, 2, D_IN), F32),
            jax.ShapeDtypeStruct((D_IN, BLOCK), BF16),
        ),
        in_specs=[pl.BlockSpec(memory_space=pltpu.HBM)] * 2,
        out_specs=[pl.BlockSpec(memory_space=V), pl.BlockSpec(memory_space=pl.ANY)],
        scratch_shapes=[
            V((8, 2, D_IN), BF16),
            V((D_IN, BLOCK), BF16),
            V((2, 8, D_IN), BF16),
            V((16, 16, D_IN), BF16),
            V((16, 16, D_IN), BF16),
            V((D_IN, BLOCK), BF16),
            V((2, BLOCK, D_IN), BF16),
            V((2, M, BLOCK), F32),
            V((M, 2 * BLOCK), BF16),
            V((2, M, BLOCK), F32),
            V((4, 32, 256), F32),
            V((4, 32, 256), BF16),
            V((3, 32, 256), BF16),
            V((32, 256), F32),
            V((32, 256), BF16),
            V((3, 32, 256), BF16),
            V((4, 32, 256), BF16),
            V((8, 128), F32),
            V((3, 8, 128), F32),
            V((8, 128), F32),
            V((3, 8, 128), F32),
            V((2, M, BLOCK), BF16),
            V((M, BLOCK), BF16),
            V((3, 4, 16, CUT), BF16),
            V((4, 16, CUT), F32),
            V((3, 4, 16, CUT), BF16),
            V((4, 16, CUT), F32),
            V((4, 16, CUT), BF16),
            V((3, 16, CUT), BF16),
            V((4, 4, 16, REST), F32),
            V((4, 4, 16, REST), BF16),
            V((3, 4, 16, REST), BF16),
            V((4, 16, REST), F32),
            V((4, 16, REST), BF16),
            V((3, 16, REST), BF16),
            V((2, 8, D_IN), F32),
            V((8, D_IN), F32),
            V((D_IN, BLOCK), F32),
            V((CHUNKS, 2, ROWS, 128), BF16),
            V((CHUNKS, 2, ROWS, 128), BF16),
            V((CHUNKS, 2, ROWS, 128), BF16),
            V((CHUNKS, 2, ROWS, 128), BF16),
            V((CHUNKS, 2, ROWS, 128), BF16),
            V((CHUNKS, 2, ROWS, 128), BF16),
            V((CHUNKS, 2, ROWS, 128), BF16),
            V((CHUNKS, 2, ROWS, 128), BF16),
            V((CHUNKS, ROWS, BLOCK), BF16),
            V((10240, 128), F32),
            pltpu.SemaphoreType.DMA,
            pltpu.SemaphoreType.DMA((NGROUPS,)),
            pltpu.SemaphoreType.DMA((4,)),
        ],
        compiler_params=pltpu.CompilerParams(
            collective_id=0, has_side_effects=True, vmem_limit_bytes=VLIM
        ),
    )(pltpu.with_memory_space_constraint(images, pltpu.HBM), pltpu.with_memory_space_constraint(weight, pltpu.HBM))
    return pl.pallas_call(
        finish,
        out_shape=(
            jax.ShapeDtypeStruct((8, 2, D_IN), F32),
            jax.ShapeDtypeStruct((D_IN, BLOCK), F32),
        ),
        in_specs=[pl.BlockSpec(memory_space=V)] * 2,
        out_specs=[pl.BlockSpec(memory_space=pl.ANY)] * 2,
        scratch_shapes=[V((D_IN, BLOCK), F32), pltpu.SemaphoreType.DMA((6,))],
        compiler_params=pltpu.CompilerParams(vmem_limit_bytes=4 * 2**20),
    )(ig, lg)


NGROUPS = 40
VLIM = 24 * 2**20


def solution(mesh):
    return jax.shard_map(
        shards,
        mesh=mesh,
        in_specs=(P(("rep", "dp"), None, None), P(None, "dp")),
        out_specs=(P(("rep", "dp"), None, None), P(None, "dp")),
        check_vma=False,
    )
```

```python
import jax
import jax.numpy as jnp
from jax import lax
from jax.experimental import pallas as pl
from jax.experimental.pallas import tpu as pltpu
from jax.sharding import PartitionSpec as P

MESH = pl.DeviceIdType.MESH
F32, BF16 = jnp.float32, jnp.bfloat16

N_REP, N_DP = 8, 32
M = 256
D_IN = 1280
BLOCK = 256
EMB = BLOCK * N_DP
S = 8192.0 / N_REP
EPS = 0.0001
INV = S * 2.0 * 25.0 / (M * EMB)
VAR = S * 25.0 / (EMB * (M - 1))
COV = S * 4.0 / (EMB * (M - 1))
CHUNKS = 4
ROWS = D_IN // 4 // CHUNKS
CUT = 1024
REST = D_IN - CUT
GRAM_UNIT = 2.0**-10


def root(t):
    return jnp.sqrt(jnp.abs(t))


def enc(v):
    return (v * jnp.abs(v)).astype(BF16)


def dec(b):
    t = b.astype(F32)
    s = root(t)
    return jnp.where(t < 0.0, -s, s)


def enc4(g):
    v = g * GRAM_UNIT
    return ((v * jnp.abs(v)) * (v * v)).astype(BF16)


def dec4(b):
    t = b.astype(F32)
    s = root(root(t)) * (1.0 / GRAM_UNIT)
    return jnp.where(t < 0.0, -s, s)


def nt(a, b):
    return lax.dot_general(a, b, (((1,), (1,)), ((), ())), preferred_element_type=F32)


def tn(a, b):
    return lax.dot_general(a, b, (((0,), (0,)), ((), ())), preferred_element_type=F32)


def nn(a, b):
    return jnp.dot(a, b, preferred_element_type=F32)


class Group:
    def __init__(self, sem):
        self.sem, self.kib = sem, 0


def kernel(
    img, w_hbm, ig, lg,
    Iv, w, I2, X, Xo, XT, Wo, WT, E, Cb, Cbo, base,
    T, Tc, Tx, Sz, Sc, Szr, TA, Dg, Dx, Ds, Dz, Dt,
    Ff,
    P32, Pc, Px, S32, Pz, Pzr, So,
    B32, Bc, Bz, B2, Bx, Bxr, Bo,
    L32, Lo, Ld, Lc, Ro, Rd, Rc, Lz, Lzr, La,
    span, send, recv, local,
):
    rep, dp = lax.axis_index("rep"), lax.axis_index("dp")
    y, zl = rep // 2, rep % 2
    c, chip = dp % 2, dp // 2
    x, zh = chip // 4, chip % 4
    o = 1 - c

    partner = (rep, chip * 2 + o)

    def at_x(k, core):
        return (rep, (((x + k) % 4) * 4 + zh) * 2 + core)

    def at_z(k, core):
        return (rep, (x * 4 + (zh + k) % 4) * 2 + core)

    def at_y(k):
        return (((y + k) % 4) * 2 + zl, dp)

    across = (y * 2 + (1 - zl), dp)

    fetch = pltpu.make_async_copy(img, Iv, local.at[0])
    fetch.start()
    wfetch = pltpu.make_async_copy(w_hbm, w, local.at[1])
    wfetch.start()
    barrier = pltpu.get_barrier_semaphore()
    peers = [partner, across]
    for k in (1, 2, 3):
        peers += [at_x(k, c), at_z(k, c), at_x(k, o), at_z(k, o), at_y(k)]
    for peer in peers:
        pl.semaphore_signal(barrier, inc=1, device_id=peer, device_id_type=MESH)
    fetch.wait()
    both = Iv[...].astype(F32)
    I2[0] = both[:, 0, :].astype(BF16)
    I2[1] = both[:, 1, :].astype(BF16)
    pl.semaphore_wait(barrier, len(peers))

    sent = Group(send)
    groups = []

    def group():
        groups.append(Group(recv.at[len(groups)]))
        return groups[-1]

    def put(src, dst, device, at=None):
        at = at or group()
        copy = pltpu.make_async_remote_copy(
            src_ref=src, dst_ref=dst, send_sem=sent.sem, recv_sem=at.sem,
            device_id=device, device_id_type=MESH,
        )
        copy.start()
        size = 1
        for n in src.shape:
            size *= n
        kib = size * jnp.dtype(src.dtype).itemsize // 1024
        at.kib += kib
        sent.kib += kib
        return at

    def wait(at):
        part = span.at[pl.ds(0, at.kib * 2)]
        pltpu.make_async_copy(part, part, at.sem).wait()

    at = pl.ds(pl.multiple_of(c * 8, 8), 8)
    A, B = pl.ds(0, CUT), pl.ds(CUT, REST)
    az, bx = {}, {}
    for k in (1, 3, 2):
        az[k], bx[k] = group(), group()
        for core in (c, o):
            put(I2.at[core, :, A], X.at[chip, at, A], at_z(k, core), az[k])
            put(I2.at[core, :, B], X.at[chip, at, B], at_x(k, core), bx[k])
    mate = put(I2.at[o], X.at[chip, at], partner)
    keep = pltpu.make_async_copy(I2.at[c], X.at[chip, at], local.at[0])
    keep.start()
    wswap = put(w_hbm, Wo, partner)
    keep.wait()
    wait(mate)
    forwards = group()
    for k in (0, 1, 3, 2):
        if k:
            wait(az[k])
        slot = x * 4 + (zh - k + 4) % 4
        for j in (2, 1, 3):
            put(X.at[slot, :, A], X.at[slot, :, A], at_x(j, c), forwards)
        if k:
            wait(bx[k])
        slot = ((x - k + 4) % 4) * 4 + zh
        for j in (2, 1, 3):
            put(X.at[slot, :, B], X.at[slot, :, B], at_z(j, c), forwards)
    wait(wswap)
    wfetch.wait()
    WT[0] = w[...].T
    WT[1] = Wo[...].T
    wait(forwards)
    xswap = put(X, Xo, partner)

    rows = X[...].reshape(M, D_IN)
    for h, wr in enumerate((w, Wo)):
        e = nn(rows, wr[...])
        E[h] = e
        Cb[:, h * BLOCK:(h + 1) * BLOCK] = (e - jnp.mean(e, axis=0, keepdims=True)).astype(BF16)
    ri = lax.broadcasted_iota(jnp.int32, (128, 128), 0)
    ci = lax.broadcasted_iota(jnp.int32, (128, 128), 1)
    top = nt(Cb[0:128, :], Cb[...])
    low = nt(Cb[128:256, :], Cb[128:256, :])
    mixed = jnp.where(ri <= ci, top[:, 0:128], low)
    T[:, :, 0:128] = mixed.reshape(4, 32, 128)
    T[:, :, 128:256] = top[:, 128:256].reshape(4, 32, 128)
    Tc[...] = enc4(T[...])
    diags = [jnp.sum(jnp.where(ri == ci, g, 0.0), axis=0, keepdims=True) for g in (top[:, 0:128], low)]
    Dg[...] = jnp.where(lax.broadcasted_iota(jnp.int32, (8, 128), 0) == 0, diags[0], diags[1])
    ts = group()
    for k in (2, 1, 3):
        put(Tc.at[(x + k) % 4], Tx.at[k - 1], at_x(k, c), ts)
        put(Dg, Dx.at[k - 1], at_x(k, c), ts)
    wait(ts)
    s = T[x] + dec4(Tx[0]) + dec4(Tx[1]) + dec4(Tx[2])
    Sz[...] = s
    Sc[...] = enc4(s)
    Ds[...] = Dg[...] + Dx[0] + Dx[1] + Dx[2]
    ss = group()
    for k in (2, 1, 3):
        put(Sc, Szr.at[k - 1], at_z(k, c), ss)
        put(Ds, Dz.at[k - 1], at_z(k, c), ss)

    def ungrammed(e, gap, cb):
        centred = e - jnp.mean(e, axis=0, keepdims=True)
        spread = jnp.sqrt(jnp.sum(centred * centred, axis=0, keepdims=True) / (M - 1) + EPS)
        pull = jnp.where(spread < 1.0, -VAR / spread, 0.0)
        diag = jnp.sum(cb * cb, axis=0, keepdims=True) / (M - 1)
        return INV * gap + pull * centred - (COV * diag) * cb

    wait(xswap)
    orows = Xo[...].reshape(M, D_IN)
    for h, wr in enumerate((w, Wo)):
        e, eo = E[h], nn(orows, wr[...])
        cb = Cb[:, h * BLOCK:(h + 1) * BLOCK].astype(F32)
        base[h] = ungrammed(e, e - eo, cb)
        if h == 0:
            cb = (eo - jnp.mean(eo, axis=0, keepdims=True)).astype(BF16)
            Cbo[...] = cb
            base[2] = ungrammed(eo, eo - e, cb.astype(F32))
    XT[0] = rows.T
    XT[1] = orows.T

    wait(ss)
    TA[c, x] = enc4(Sz[...] + dec4(Szr[0]) + dec4(Szr[1]) + dec4(Szr[2]))
    gs = group()
    for k in (2, 1, 3):
        for core in (c, o):
            put(TA.at[c, x], TA.at[c, x], at_x(k, core), gs)
    put(TA.at[c, x], TA.at[c, x], partner, gs)
    Dt[c] = Ds[...] + Dz[0] + Dz[1] + Dz[2]
    put(Dt.at[c], Dt.at[c], partner, gs)
    wait(gs)
    def gram_of(view):
        mixed = dec4(TA[view, :, :, 0:128].reshape(128, 128))
        side = dec4(TA[view, :, :, 128:256].reshape(128, 128))
        flip = mixed.T
        ga = jnp.where(ri == ci, Dt[view, 0:1], jnp.where(ri < ci, mixed, flip))
        gd = jnp.where(ri == ci, Dt[view, 1:2], jnp.where(ri > ci, mixed, flip))
        gram = jnp.concatenate(
            [jnp.concatenate([ga, side], axis=1), jnp.concatenate([side.T, gd], axis=1)], axis=0
        )
        hi = gram.astype(BF16)
        return hi, (gram - hi.astype(F32)).astype(BF16)

    def feature_grad(gram, cb, rest):
        through = nn(gram[0], cb) + nn(gram[1], cb)
        return (rest + through * (COV / (M - 1))).astype(BF16)

    gram = gram_of(c)
    Ff[0] = feature_grad(gram, Cb[:, 0:BLOCK], base[0])
    L32[...] = nn(XT[0], Ff[0]) + nn(XT[1], feature_grad(gram_of(o), Cbo[...], base[2]))

    def rows_of(k, q):
        return pl.ds(pl.multiple_of(((y + k) % 4) * 320 + q * ROWS, ROWS), ROWS)

    sides = (pl.ds(0, 128), pl.ds(128, 128))
    ways = (1, 3)
    opp, direct, joint = {}, {}, {}
    for q in range(CHUNKS):
        opp[q], direct[q] = group(), group()
        for i in range(2):
            Lo[q, i] = enc(L32[rows_of(2, q), sides[i]])
            put(Lo.at[q, i], Ro.at[q, i], at_y(ways[i]), opp[q])

    def send_direct(q):
        for i in range(2):
            Ld[q, i] = enc(L32[rows_of(ways[i], q), sides[1 - i]])
            put(Ld.at[q, i], Rd.at[q, 1 - i], at_y(ways[i]), direct[q])

    send_direct(0)
    Ff[1] = feature_grad(gram, Cb[:, BLOCK:2 * BLOCK], base[1])
    part = nn(Ff[0], WT[0]) + nn(Ff[1], WT[1])
    P32[...] = part[:, 0:CUT].reshape(4, 4, 16, CUT)
    part = part[:, CUT:D_IN].reshape(4, 4, 16, REST)
    halves = (pl.ds(0, CUT // 2), pl.ds(CUT // 2, CUT // 2))
    Pc[...] = enc(P32[...])
    for j in range(4):
        B32[j] = part[:, j]
        Bc[j] = enc(part[:, j])
    ps = [group(), group()]
    bz = group()
    for i in range(2):
        for k in (2, 1, 3):
            put(Pc.at[(x + k) % 4, :, :, halves[i]], Px.at[k - 1, :, :, halves[i]], at_x(k, c), ps[i])
        if i == 0:
            for k in (2, 1, 3):
                put(Bc.at[(zh + k) % 4], Bz.at[k - 1], at_z(k, c), bz)
    for q in range(CHUNKS):
        wait(opp[q])
        for i in range(2):
            Lc[q, i] = enc(L32[rows_of(ways[i], q), sides[i]] + dec(Ro[q, i]))
            put(Lc.at[q, i], Rc.at[q, i], at_y(ways[i]), direct[q])
        if q + 1 < CHUNKS:
            send_direct(q + 1)

    def at_core(core):
        return pl.ds(pl.multiple_of(core * 8, 8), 8)

    mates = group()

    def sum_a(i):
        wait(ps[i])
        cols = halves[i]
        for j in range(4):
            s = P32[x, j, :, cols] + dec(Px[0, j, :, cols]) + dec(Px[1, j, :, cols]) + dec(Px[2, j, :, cols])
            S32[j, :, cols] = s
            Pz[j, :, cols] = enc(s)
        at = group()
        for k in (2, 1, 3):
            for core in (c, o):
                put(Pz.at[(zh + k) % 4, at_core(core), cols], Pzr.at[k - 1, c, :, cols], at_z(k, core), at)
        put(S32.at[zh, at_core(o), cols], So.at[:, cols], partner, mates)
        return at

    def sum_b():
        wait(bz)
        for j in range(4):
            s = B32[zh, j] + dec(Bz[0, j]) + dec(Bz[1, j]) + dec(Bz[2, j])
            B2[j] = s
            Bx[j] = enc(s)
        at = group()
        for k in (2, 1, 3):
            for core in (c, o):
                put(Bx.at[(x + k) % 4, at_core(core)], Bxr.at[k - 1, c], at_x(k, core), at)
        put(B2.at[x, at_core(o)], Bo, partner, mates)
        return at

    zz, ls, kept = {}, {}, []
    last = group()

    def sum_l(q):
        wait(direct[q])
        for i in range(2):
            Lz[q, i] = enc(L32[rows_of(0, q), sides[i]] + dec(Rd[q, i]) + dec(Rc[q, i]))
        zz[q] = put(Lz.at[q], Lzr.at[q], across)

    def share_l(q):
        wait(zz[q])
        for i in range(2):
            La[q, :, sides[i]] = enc(dec(Lz[q, i]) + dec(Lzr[q, i]))
        here = lg.at[rows_of(0, q)]
        for k in (2, 1, 3):
            put(La.at[q], here, at_y(k), last)
        kept.append(pltpu.make_async_copy(La.at[q], here, local.at[q]))
        kept[-1].start()

    def forward_l(q):
        pass

    pz = []
    sum_l(0)
    sum_l(1)
    sum_l(2)
    share_l(0)
    sum_l(3)
    share_l(1)
    pz.append(sum_a(0))
    bs = sum_b()
    pz.append(sum_a(1))
    share_l(2)
    share_l(3)

    wait(mates)
    mine = at_core(c)

    def total(view, first, second):
        a, b = first, second
        for k in range(3):
            a = a + dec(Pzr[k, view])
            b = b + dec(Bxr[k, view])
        return jnp.concatenate([a, b], axis=1)

    wait(pz[0])
    wait(pz[1])
    wait(bs)
    own = total(c, S32[zh, mine], B2[x, mine])
    other = total(o, So[...], Bo[...])
    first = c == 0
    ig[:, 0, :] = jnp.where(first, own, other)
    ig[:, 1, :] = jnp.where(first, other, own)

    wait(last)
    for copy in kept:
        copy.wait()
    wait(sent)


def finish(ig, lg, image_grad, weight_grad, full, sem):
    copies = [pltpu.make_async_copy(ig, image_grad, sem.at[0])]
    copies[0].start()
    for j in range(5):
        at = pl.ds(j * 256, 256)
        full[at] = dec(lg[at])
        copies.append(pltpu.make_async_copy(full.at[at], weight_grad.at[at], sem.at[1 + j]))
        copies[-1].start()
    for copy in copies:
        copy.wait()


def shards(images, weight):
    V = pltpu.VMEM
    ig, lg = pl.pallas_call(
        kernel,
        out_shape=(
            jax.ShapeDtypeStruct((8, 2, D_IN), F32),
            jax.ShapeDtypeStruct((D_IN, BLOCK), BF16),
        ),
        in_specs=[pl.BlockSpec(memory_space=pltpu.HBM)] * 2,
        out_specs=[pl.BlockSpec(memory_space=V), pl.BlockSpec(memory_space=pl.ANY)],
        scratch_shapes=[
            V((8, 2, D_IN), BF16),
            V((D_IN, BLOCK), BF16),
            V((2, 8, D_IN), BF16),
            V((16, 16, D_IN), BF16),
            V((16, 16, D_IN), BF16),
            V((2, D_IN, M), BF16),
            V((D_IN, BLOCK), BF16),
            V((2, BLOCK, D_IN), BF16),
            V((2, M, BLOCK), F32),
            V((M, 2 * BLOCK), BF16),
            V((M, BLOCK), BF16),
            V((3, M, BLOCK), F32),
            V((4, 32, 256), F32),
            V((4, 32, 256), BF16),
            V((3, 32, 256), BF16),
            V((32, 256), F32),
            V((32, 256), BF16),
            V((3, 32, 256), BF16),
            V((2, 4, 32, 256), BF16),
            V((8, 128), F32),
            V((3, 8, 128), F32),
            V((8, 128), F32),
            V((3, 8, 128), F32),
            V((2, 8, 128), F32),
            V((2, M, BLOCK), BF16),
            V((4, 4, 16, CUT), F32),
            V((4, 4, 16, CUT), BF16),
            V((3, 4, 16, CUT), BF16),
            V((4, 16, CUT), F32),
            V((4, 16, CUT), BF16),
            V((3, 2, 8, CUT), BF16),
            V((8, CUT), F32),
            V((4, 4, 16, REST), F32),
            V((4, 4, 16, REST), BF16),
            V((3, 4, 16, REST), BF16),
            V((4, 16, REST), F32),
            V((4, 16, REST), BF16),
            V((3, 2, 8, REST), BF16),
            V((8, REST), F32),
            V((D_IN, BLOCK), F32),
            V((CHUNKS, 2, ROWS, 128), BF16),
            V((CHUNKS, 2, ROWS, 128), BF16),
            V((CHUNKS, 2, ROWS, 128), BF16),
            V((CHUNKS, 2, ROWS, 128), BF16),
            V((CHUNKS, 2, ROWS, 128), BF16),
            V((CHUNKS, 2, ROWS, 128), BF16),
            V((CHUNKS, 2, ROWS, 128), BF16),
            V((CHUNKS, 2, ROWS, 128), BF16),
            V((CHUNKS, ROWS, BLOCK), BF16),
            V((10240, 128), F32),
            pltpu.SemaphoreType.DMA,
            pltpu.SemaphoreType.DMA((NGROUPS,)),
            pltpu.SemaphoreType.DMA((4,)),
        ],
        compiler_params=pltpu.CompilerParams(
            collective_id=0, has_side_effects=True, vmem_limit_bytes=VLIM
        ),
    )(pltpu.with_memory_space_constraint(images, pltpu.HBM), pltpu.with_memory_space_constraint(weight, pltpu.HBM))
    return pl.pallas_call(
        finish,
        out_shape=(
            jax.ShapeDtypeStruct((8, 2, D_IN), F32),
            jax.ShapeDtypeStruct((D_IN, BLOCK), F32),
        ),
        in_specs=[pl.BlockSpec(memory_space=V)] * 2,
        out_specs=[pl.BlockSpec(memory_space=pl.ANY)] * 2,
        scratch_shapes=[V((D_IN, BLOCK), F32), pltpu.SemaphoreType.DMA((6,))],
        compiler_params=pltpu.CompilerParams(vmem_limit_bytes=4 * 2**20),
    )(ig, lg)


NGROUPS = 40
VLIM = 24 * 2**20


def solution(mesh):
    return jax.shard_map(
        shards,
        mesh=mesh,
        in_specs=(P(("rep", "dp"), None, None), P(None, "dp")),
        out_specs=(P(("rep", "dp"), None, None), P(None, "dp")),
        check_vma=False,
    )
```

```python
import jax
import jax.numpy as jnp
from jax import lax
from jax.experimental import pallas as pl
from jax.experimental.pallas import tpu as pltpu
from jax.sharding import PartitionSpec as P

MESH = pl.DeviceIdType.MESH
F32, BF16 = jnp.float32, jnp.bfloat16

N_REP, N_DP = 8, 32
M = 256
D_IN = 1280
BLOCK = 256
EMB = BLOCK * N_DP
S = 8192.0 / N_REP
EPS = 0.0001
INV = S * 2.0 * 25.0 / (M * EMB)
VAR = S * 25.0 / (EMB * (M - 1))
COV = S * 4.0 / (EMB * (M - 1))
CHUNKS = 4
ROWS = D_IN // 4 // CHUNKS
CUT = 1024
REST = D_IN - CUT
PCUT = 1024
PREST = D_IN - PCUT
GRAM_UNIT = 2.0**-10


def root(t):
    return jnp.sqrt(jnp.abs(t))


def enc(v):
    return (v * jnp.abs(v)).astype(BF16)


def dec(b):
    t = b.astype(F32)
    s = root(t)
    return jnp.where(t < 0.0, -s, s)


def enc4(g):
    v = g * GRAM_UNIT
    return ((v * jnp.abs(v)) * (v * v)).astype(BF16)


def dec4(b):
    t = b.astype(F32)
    s = root(root(t)) * (1.0 / GRAM_UNIT)
    return jnp.where(t < 0.0, -s, s)


def nt(a, b):
    return lax.dot_general(a, b, (((1,), (1,)), ((), ())), preferred_element_type=F32)


def tn(a, b):
    return lax.dot_general(a, b, (((0,), (0,)), ((), ())), preferred_element_type=F32)


def nn(a, b):
    return jnp.dot(a, b, preferred_element_type=F32)


class Group:
    def __init__(self, sem):
        self.sem, self.kib = sem, 0


def kernel(
    img, w_hbm, ig, lg,
    Iv, w, I2, X, Xo, XT, Wo, WT, E, Cb, Cbo, base,
    T, Tc, Tx, Sz, Sc, Szr, TA, Dg, Dx, Ds, Dz, Dt,
    Ff,
    P32, Pc, Px, S32, Pz, Pzr, So,
    B32, Bc, Bz, B2, Bx, Bxr, Bo,
    L32, Ly, Lr, Lz, Lzr, La,
    span, send, recv, local, near,
):
    rep, dp = lax.axis_index("rep"), lax.axis_index("dp")
    y, zl = rep // 2, rep % 2
    c, chip = dp % 2, dp // 2
    x, zh = chip // 4, chip % 4
    o = 1 - c

    partner = (rep, chip * 2 + o)

    def at_x(k, core):
        return (rep, (((x + k) % 4) * 4 + zh) * 2 + core)

    def at_z(k, core):
        return (rep, (x * 4 + (zh + k) % 4) * 2 + core)

    def at_y(k):
        return (((y + k) % 4) * 2 + zl, dp)

    across = (y * 2 + (1 - zl), dp)

    fetch = pltpu.make_async_copy(img, Iv, local.at[0])
    fetch.start()
    wfetch = pltpu.make_async_copy(w_hbm, w, local.at[1])
    wfetch.start()
    barrier = pltpu.get_barrier_semaphore()
    peers = [partner, across]
    for k in (1, 2, 3):
        peers += [at_x(k, c), at_x(k, o), at_y(k)]
    for k in (1, 3):
        peers += [at_z(k, c), at_z(k, o)]
    for peer in peers:
        pl.semaphore_signal(barrier, inc=1, device_id=peer, device_id_type=MESH)
    fetch.wait()
    both = Iv[...].astype(F32)
    I2[0] = both[:, 0, :].astype(BF16)
    I2[1] = both[:, 1, :].astype(BF16)
    pl.semaphore_wait(barrier, len(peers))
    pl.semaphore_signal(near, inc=1, device_id=at_z(1, c), device_id_type=MESH)

    sent = Group(send)
    groups = []

    def group():
        groups.append(Group(recv.at[len(groups)]))
        return groups[-1]

    def put(src, dst, device, at=None):
        at = at or group()
        copy = pltpu.make_async_remote_copy(
            src_ref=src, dst_ref=dst, send_sem=sent.sem, recv_sem=at.sem,
            device_id=device, device_id_type=MESH,
        )
        copy.start()
        size = 1
        for n in src.shape:
            size *= n
        kib = size * jnp.dtype(src.dtype).itemsize // 1024
        at.kib += kib
        sent.kib += kib
        return at

    def wait(at):
        part = span.at[pl.ds(0, at.kib * 2)]
        pltpu.make_async_copy(part, part, at.sem).wait()

    at = pl.ds(pl.multiple_of(c * 8, 8), 8)
    A, B = pl.ds(0, CUT), pl.ds(CUT, REST)
    az, bx = {}, {}
    for k in (1, 3, 2):
        az[k], bx[k] = group(), group()
        for core in (c, o):
            if k != 2:
                put(I2.at[core, :, A], X.at[chip, at, A], at_z(k, core), az[k])
            put(I2.at[core, :, B], X.at[chip, at, B], at_x(k, core), bx[k])
    mate = put(I2.at[o], X.at[chip, at], partner)
    keep = pltpu.make_async_copy(I2.at[c], X.at[chip, at], local.at[0])
    keep.start()
    wswap = put(w_hbm, Wo, partner)
    keep.wait()
    wait(mate)
    forwards = group()
    pl.semaphore_wait(near, 1)
    for core in (c, o):
        put(I2.at[core, :, A], X.at[chip, at, A], at_z(2, core), az[2])
    for k in (0, 1, 3, 2):
        if k:
            wait(az[k])
        slot = x * 4 + (zh - k + 4) % 4
        for j in (2, 1, 3):
            put(X.at[slot, :, A], X.at[slot, :, A], at_x(j, c), forwards)
        if k:
            wait(bx[k])
        slot = ((x - k + 4) % 4) * 4 + zh
        for j in (2, 1, 3):
            put(X.at[slot, :, B], X.at[slot, :, B], at_z(j, c), forwards)
    wait(wswap)
    wfetch.wait()
    WT[0] = w[...].T
    WT[1] = Wo[...].T
    wait(forwards)
    xswap = put(X, Xo, partner)

    rows = X[...].reshape(M, D_IN)
    for h, wr in enumerate((w, Wo)):
        e = nn(rows, wr[...])
        E[h] = e
        Cb[:, h * BLOCK:(h + 1) * BLOCK] = (e - jnp.mean(e, axis=0, keepdims=True)).astype(BF16)
    ri = lax.broadcasted_iota(jnp.int32, (128, 128), 0)
    ci = lax.broadcasted_iota(jnp.int32, (128, 128), 1)
    top = nt(Cb[0:128, :], Cb[...])
    low = nt(Cb[128:256, :], Cb[128:256, :])
    mixed = jnp.where(ri <= ci, top[:, 0:128], low)
    T[:, :, 0:128] = mixed.reshape(4, 32, 128)
    T[:, :, 128:256] = top[:, 128:256].reshape(4, 32, 128)
    Tc[...] = enc4(T[...])
    diags = [jnp.sum(jnp.where(ri == ci, g, 0.0), axis=0, keepdims=True) for g in (top[:, 0:128], low)]
    Dg[...] = jnp.where(lax.broadcasted_iota(jnp.int32, (8, 128), 0) == 0, diags[0], diags[1])
    ts = group()
    for k in (2, 1, 3):
        put(Tc.at[(x + k) % 4], Tx.at[k - 1], at_x(k, c), ts)
        put(Dg, Dx.at[k - 1], at_x(k, c), ts)
    wait(ts)
    s = T[x] + dec4(Tx[0]) + dec4(Tx[1]) + dec4(Tx[2])
    Sz[...] = s
    Sc[...] = enc4(s)
    Ds[...] = Dg[...] + Dx[0] + Dx[1] + Dx[2]
    ss = group()
    for k in (2, 1, 3):
        put(Sc, Szr.at[k - 1], at_z(k, c), ss)
        put(Ds, Dz.at[k - 1], at_z(k, c), ss)

    def ungrammed(e, gap, cb):
        centred = e - jnp.mean(e, axis=0, keepdims=True)
        spread = jnp.sqrt(jnp.sum(centred * centred, axis=0, keepdims=True) / (M - 1) + EPS)
        pull = jnp.where(spread < 1.0, -VAR / spread, 0.0)
        diag = jnp.sum(cb * cb, axis=0, keepdims=True) / (M - 1)
        return INV * gap + pull * centred - (COV * diag) * cb

    wait(xswap)
    orows = Xo[...].reshape(M, D_IN)
    for h, wr in enumerate((w, Wo)):
        e, eo = E[h], nn(orows, wr[...])
        cb = Cb[:, h * BLOCK:(h + 1) * BLOCK].astype(F32)
        base[h] = ungrammed(e, e - eo, cb)
        if h == 0:
            cb = (eo - jnp.mean(eo, axis=0, keepdims=True)).astype(BF16)
            Cbo[...] = cb
            base[2] = ungrammed(eo, eo - e, cb.astype(F32))
    XT[0] = rows.T
    XT[1] = orows.T

    wait(ss)
    TA[c, x] = enc4(Sz[...] + dec4(Szr[0]) + dec4(Szr[1]) + dec4(Szr[2]))
    gs, go = group(), group()
    for core, at in ((c, gs), (o, go)):
        for k in (2, 1, 3):
            put(TA.at[c, x], TA.at[c, x], at_x(k, core), at)
    put(TA.at[c, x], TA.at[c, x], partner, go)
    Dt[c] = Ds[...] + Dz[0] + Dz[1] + Dz[2]
    put(Dt.at[c], Dt.at[c], partner, go)
    wait(gs)
    def gram_of(view):
        mixed = dec4(TA[view, :, :, 0:128].reshape(128, 128))
        side = dec4(TA[view, :, :, 128:256].reshape(128, 128))
        flip = mixed.T
        ga = jnp.where(ri == ci, Dt[view, 0:1], jnp.where(ri < ci, mixed, flip))
        gd = jnp.where(ri == ci, Dt[view, 1:2], jnp.where(ri > ci, mixed, flip))
        gram = jnp.concatenate(
            [jnp.concatenate([ga, side], axis=1), jnp.concatenate([side.T, gd], axis=1)], axis=0
        )
        hi = gram.astype(BF16)
        return hi, (gram - hi.astype(F32)).astype(BF16)

    def feature_grad(gram, cb, rest):
        through = nn(gram[0], cb) + nn(gram[1], cb)
        return (rest + through * (COV / (M - 1))).astype(BF16)

    gram = gram_of(c)
    Ff[0] = feature_grad(gram, Cb[:, 0:BLOCK], base[0])
    Ff[1] = feature_grad(gram, Cb[:, BLOCK:2 * BLOCK], base[1])
    part = nn(Ff[0], WT[0]) + nn(Ff[1], WT[1])
    P32[...] = part[:, 0:PCUT].reshape(4, 4, 16, PCUT)
    part = part[:, PCUT:D_IN].reshape(4, 4, 16, PREST)
    halves = (pl.ds(0, PCUT // 2), pl.ds(PCUT // 2, PCUT // 2))
    Pc[...] = enc(P32[...])
    for j in range(4):
        B32[j] = part[:, j]
        Bc[j] = enc(part[:, j])
    L32[...] = nn(XT[0], Ff[0])

    wait(go)
    L32[...] += nn(XT[1], feature_grad(gram_of(o), Cbo[...], base[2]))

    def rows_of(k, q):
        return pl.ds(pl.multiple_of(((y + k) % 4) * 320 + q * ROWS, ROWS), ROWS)

    sides = (pl.ds(0, 128), pl.ds(128, 128))
    direct = {}
    for q in range(CHUNKS):
        direct[q] = group()
        for k in (2, 1, 3):
            for i in range(2):
                Ly[q, k - 1, i] = enc(L32[rows_of(k, q), sides[i]])
            put(Ly.at[q, k - 1], Lr.at[q, k - 1], at_y(k), direct[q])
    ps = [group(), group()]
    bz = group()
    for i in range(2):
        for k in (2, 1, 3):
            put(Pc.at[(x + k) % 4, :, :, halves[i]], Px.at[k - 1, :, :, halves[i]], at_x(k, c), ps[i])
        if i == 0:
            for k in (2, 1, 3):
                put(Bc.at[(zh + k) % 4], Bz.at[k - 1], at_z(k, c), bz)
    def at_core(core):
        return pl.ds(pl.multiple_of(core * 8, 8), 8)

    mates = group()

    def sum_a(i):
        wait(ps[i])
        cols = halves[i]
        for j in range(4):
            s = P32[x, j, :, cols] + dec(Px[0, j, :, cols]) + dec(Px[1, j, :, cols]) + dec(Px[2, j, :, cols])
            S32[j, :, cols] = s
            Pz[j, :, cols] = enc(s)
        at = group()
        for k in (2, 1, 3):
            for core in (c, o):
                put(Pz.at[(zh + k) % 4, at_core(core), cols], Pzr.at[k - 1, c, :, cols], at_z(k, core), at)
        put(S32.at[zh, at_core(o), cols], So.at[:, cols], partner, mates)
        return at

    def sum_b():
        wait(bz)
        for j in range(4):
            s = B32[zh, j] + dec(Bz[0, j]) + dec(Bz[1, j]) + dec(Bz[2, j])
            B2[j] = s
            Bx[j] = enc(s)
        at = group()
        for k in (2, 1, 3):
            for core in (c, o):
                put(Bx.at[(x + k) % 4, at_core(core)], Bxr.at[k - 1, c], at_x(k, core), at)
        put(B2.at[x, at_core(o)], Bo, partner, mates)
        return at

    zz, kept = {}, []
    last = group()

    def sum_l(q):
        wait(direct[q])
        for i in range(2):
            Lz[q, i] = enc(L32[rows_of(0, q), sides[i]] + dec(Lr[q, 0, i]) + dec(Lr[q, 1, i]) + dec(Lr[q, 2, i]))
        zz[q] = put(Lz.at[q], Lzr.at[q], across)

    def share_l(q):
        wait(zz[q])
        for i in range(2):
            La[q, :, sides[i]] = enc(dec(Lz[q, i]) + dec(Lzr[q, i]))
        here = lg.at[rows_of(0, q)]
        for k in (2, 1, 3):
            put(La.at[q], here, at_y(k), last)
        kept.append(pltpu.make_async_copy(La.at[q], here, local.at[q]))
        kept[-1].start()

    pz = []
    sum_l(0)
    sum_l(1)
    pz.append(sum_a(0))
    bs = sum_b()
    share_l(0)
    sum_l(2)
    pz.append(sum_a(1))
    share_l(1)
    sum_l(3)
    share_l(2)
    share_l(3)

    wait(mates)
    mine = at_core(c)

    def total(view, first, second):
        a, b = first, second
        for k in range(3):
            a = a + dec(Pzr[k, view])
            b = b + dec(Bxr[k, view])
        return jnp.concatenate([a, b], axis=1)

    wait(pz[0])
    wait(pz[1])
    wait(bs)
    own = total(c, S32[zh, mine], B2[x, mine])
    other = total(o, So[...], Bo[...])
    first = c == 0
    ig[:, 0, :] = jnp.where(first, own, other)
    ig[:, 1, :] = jnp.where(first, other, own)

    wait(last)
    for copy in kept:
        copy.wait()
    wait(sent)


def finish(ig, lg, image_grad, weight_grad, full, sem):
    copies = [pltpu.make_async_copy(ig, image_grad, sem.at[0])]
    copies[0].start()
    for j in range(5):
        at = pl.ds(j * 256, 256)
        full[at] = dec(lg[at])
        copies.append(pltpu.make_async_copy(full.at[at], weight_grad.at[at], sem.at[1 + j]))
        copies[-1].start()
    for copy in copies:
        copy.wait()


def shards(images, weight):
    V = pltpu.VMEM
    ig, lg = pl.pallas_call(
        kernel,
        out_shape=(
            jax.ShapeDtypeStruct((8, 2, D_IN), F32),
            jax.ShapeDtypeStruct((D_IN, BLOCK), BF16),
        ),
        in_specs=[pl.BlockSpec(memory_space=pltpu.HBM)] * 2,
        out_specs=[pl.BlockSpec(memory_space=V), pl.BlockSpec(memory_space=pl.ANY)],
        scratch_shapes=[
            V((8, 2, D_IN), BF16),
            V((D_IN, BLOCK), BF16),
            V((2, 8, D_IN), BF16),
            V((16, 16, D_IN), BF16),
            V((16, 16, D_IN), BF16),
            V((2, D_IN, M), BF16),
            V((D_IN, BLOCK), BF16),
            V((2, BLOCK, D_IN), BF16),
            V((2, M, BLOCK), F32),
            V((M, 2 * BLOCK), BF16),
            V((M, BLOCK), BF16),
            V((3, M, BLOCK), F32),
            V((4, 32, 256), F32),
            V((4, 32, 256), BF16),
            V((3, 32, 256), BF16),
            V((32, 256), F32),
            V((32, 256), BF16),
            V((3, 32, 256), BF16),
            V((2, 4, 32, 256), BF16),
            V((8, 128), F32),
            V((3, 8, 128), F32),
            V((8, 128), F32),
            V((3, 8, 128), F32),
            V((2, 8, 128), F32),
            V((2, M, BLOCK), BF16),
            V((4, 4, 16, PCUT), F32),
            V((4, 4, 16, PCUT), BF16),
            V((3, 4, 16, PCUT), BF16),
            V((4, 16, PCUT), F32),
            V((4, 16, PCUT), BF16),
            V((3, 2, 8, PCUT), BF16),
            V((8, PCUT), F32),
            V((4, 4, 16, PREST), F32),
            V((4, 4, 16, PREST), BF16),
            V((3, 4, 16, PREST), BF16),
            V((4, 16, PREST), F32),
            V((4, 16, PREST), BF16),
            V((3, 2, 8, PREST), BF16),
            V((8, PREST), F32),
            V((D_IN, BLOCK), F32),
            V((CHUNKS, 3, 2, ROWS, 128), BF16),
            V((CHUNKS, 3, 2, ROWS, 128), BF16),
            V((CHUNKS, 2, ROWS, 128), BF16),
            V((CHUNKS, 2, ROWS, 128), BF16),
            V((CHUNKS, ROWS, BLOCK), BF16),
            V((10240, 128), F32),
            pltpu.SemaphoreType.DMA,
            pltpu.SemaphoreType.DMA((NGROUPS,)),
            pltpu.SemaphoreType.DMA((4,)),
            pltpu.SemaphoreType.REGULAR,
        ],
        compiler_params=pltpu.CompilerParams(
            collective_id=0, has_side_effects=True, vmem_limit_bytes=VLIM
        ),
    )(pltpu.with_memory_space_constraint(images, pltpu.HBM), pltpu.with_memory_space_constraint(weight, pltpu.HBM))
    return pl.pallas_call(
        finish,
        out_shape=(
            jax.ShapeDtypeStruct((8, 2, D_IN), F32),
            jax.ShapeDtypeStruct((D_IN, BLOCK), F32),
        ),
        in_specs=[pl.BlockSpec(memory_space=V)] * 2,
        out_specs=[pl.BlockSpec(memory_space=pl.ANY)] * 2,
        scratch_shapes=[V((D_IN, BLOCK), F32), pltpu.SemaphoreType.DMA((6,))],
        compiler_params=pltpu.CompilerParams(vmem_limit_bytes=4 * 2**20),
    )(ig, lg)


NGROUPS = 40
VLIM = 24 * 2**20


def solution(mesh):
    return jax.shard_map(
        shards,
        mesh=mesh,
        in_specs=(P(("rep", "dp"), None, None), P(None, "dp")),
        out_specs=(P(("rep", "dp"), None, None), P(None, "dp")),
        check_vma=False,
    )
```

```python
import jax
import jax.numpy as jnp
from jax import lax
from jax.experimental import pallas as pl
from jax.experimental.pallas import tpu as pltpu
from jax.sharding import PartitionSpec as P

MESH = pl.DeviceIdType.MESH
F32, BF16 = jnp.float32, jnp.bfloat16

N_REP, N_DP = 8, 32
M = 256
D_IN = 1280
BLOCK = 256
EMB = BLOCK * N_DP
S = 8192.0 / N_REP
EPS = 0.0001
INV = S * 2.0 * 25.0 / (M * EMB)
VAR = S * 25.0 / (EMB * (M - 1))
COV = S * 4.0 / (EMB * (M - 1))
PIECE = D_IN // 4
SIZES = (64, 96, 96, 64)
CHUNKS = len(SIZES)
CUT = 896
REST = D_IN - CUT
PCUT = 1024
PREST = D_IN - PCUT
GRAM_UNIT = 2.0**-10


def root(t):
    return jnp.sqrt(jnp.abs(t))


def enc(v):
    return (v * jnp.abs(v)).astype(BF16)


def dec(b):
    t = b.astype(F32)
    s = root(t)
    return jnp.where(t < 0.0, -s, s)


def enc4(g):
    v = g * GRAM_UNIT
    return ((v * jnp.abs(v)) * (v * v)).astype(BF16)


def dec4(b):
    t = b.astype(F32)
    s = root(root(t)) * (1.0 / GRAM_UNIT)
    return jnp.where(t < 0.0, -s, s)


def nt(a, b):
    return lax.dot_general(a, b, (((1,), (1,)), ((), ())), preferred_element_type=F32)


def tn(a, b):
    return lax.dot_general(a, b, (((0,), (0,)), ((), ())), preferred_element_type=F32)


def nn(a, b):
    return jnp.dot(a, b, preferred_element_type=F32)


class Group:
    def __init__(self, sem):
        self.sem, self.kib = sem, 0


def kernel(
    img, w_hbm, ig, lg,
    Iv, w, I2, X, Xo, XT, Wo, WT, E, Cb, Cbo, base,
    T, Tc, Tx, Sz, Sc, Szr, TA, Dg, Dx, Ds, Dz, Dt,
    Ff,
    P32, Pc, Px, S32, Pz, Pzr, So,
    B32, Bc, Bz, B2, Bx, Bxr, Bo,
    L32, Ly, Lr, Lz, Lzr, La,
    span, send, recv, local, near,
):
    rep, dp = lax.axis_index("rep"), lax.axis_index("dp")
    y, zl = rep // 2, rep % 2
    c, chip = dp % 2, dp // 2
    x, zh = chip // 4, chip % 4
    o = 1 - c

    partner = (rep, chip * 2 + o)

    def at_x(k, core):
        return (rep, (((x + k) % 4) * 4 + zh) * 2 + core)

    def at_z(k, core):
        return (rep, (x * 4 + (zh + k) % 4) * 2 + core)

    def at_y(k):
        return (((y + k) % 4) * 2 + zl, dp)

    across = (y * 2 + (1 - zl), dp)

    fetch = pltpu.make_async_copy(img, Iv, local.at[0])
    fetch.start()
    wfetch = pltpu.make_async_copy(w_hbm, w, local.at[1])
    wfetch.start()
    barrier = pltpu.get_barrier_semaphore()
    peers = [partner, across]
    for k in (1, 2, 3):
        peers += [at_x(k, c), at_x(k, o), at_y(k)]
    for k in (1, 3):
        peers += [at_z(k, c), at_z(k, o)]
    for peer in peers:
        pl.semaphore_signal(barrier, inc=1, device_id=peer, device_id_type=MESH)
    fetch.wait()
    both = Iv[...].astype(F32)
    I2[0] = both[:, 0, :].astype(BF16)
    I2[1] = both[:, 1, :].astype(BF16)
    pl.semaphore_wait(barrier, len(peers))
    pl.semaphore_signal(near, inc=1, device_id=at_z(1, c), device_id_type=MESH)

    sent = Group(send)
    groups = []

    def group():
        groups.append(Group(recv.at[len(groups)]))
        return groups[-1]

    def put(src, dst, device, at=None):
        at = at or group()
        copy = pltpu.make_async_remote_copy(
            src_ref=src, dst_ref=dst, send_sem=sent.sem, recv_sem=at.sem,
            device_id=device, device_id_type=MESH,
        )
        copy.start()
        size = 1
        for n in src.shape:
            size *= n
        kib = size * jnp.dtype(src.dtype).itemsize // 1024
        at.kib += kib
        sent.kib += kib
        return at

    def wait(at):
        part = span.at[pl.ds(0, at.kib * 2)]
        pltpu.make_async_copy(part, part, at.sem).wait()

    at = pl.ds(pl.multiple_of(c * 8, 8), 8)
    A, B = pl.ds(0, CUT), pl.ds(CUT, REST)
    az, bx = {}, {}
    for k in (1, 3, 2):
        az[k], bx[k] = group(), group()
        for core in (c, o):
            if k != 2:
                put(I2.at[core, :, A], X.at[chip, at, A], at_z(k, core), az[k])
            put(I2.at[core, :, B], X.at[chip, at, B], at_x(k, core), bx[k])
    mate = put(I2.at[o], X.at[chip, at], partner)
    keep = pltpu.make_async_copy(I2.at[c], X.at[chip, at], local.at[0])
    keep.start()
    wswap = put(w_hbm, Wo, partner)
    keep.wait()
    wait(mate)
    forwards = group()
    pl.semaphore_wait(near, 1)
    for core in (c, o):
        put(I2.at[core, :, A], X.at[chip, at, A], at_z(2, core), az[2])
    for name, k in (("A", 0), ("B", 0), ("B", 1), ("B", 3), ("A", 1), ("A", 3), ("B", 2), ("A", 2)):
        if name == "A":
            if k:
                wait(az[k])
            slot = x * 4 + (zh - k + 4) % 4
            for j in (2, 1, 3):
                put(X.at[slot, :, A], X.at[slot, :, A], at_x(j, c), forwards)
        else:
            if k:
                wait(bx[k])
            slot = ((x - k + 4) % 4) * 4 + zh
            for j in (2, 1, 3):
                put(X.at[slot, :, B], X.at[slot, :, B], at_z(j, c), forwards)
    wait(wswap)
    wfetch.wait()
    WT[0] = w[...].T
    WT[1] = Wo[...].T
    wait(forwards)
    xswap = put(X, Xo, partner)

    rows = X[...].reshape(M, D_IN)
    for h, wr in enumerate((w, Wo)):
        e = nn(rows, wr[...])
        E[h] = e
        Cb[:, h * BLOCK:(h + 1) * BLOCK] = (e - jnp.mean(e, axis=0, keepdims=True)).astype(BF16)
    ri = lax.broadcasted_iota(jnp.int32, (128, 128), 0)
    ci = lax.broadcasted_iota(jnp.int32, (128, 128), 1)
    top = nt(Cb[0:128, :], Cb[...])
    low = nt(Cb[128:256, :], Cb[128:256, :])
    mixed = jnp.where(ri <= ci, top[:, 0:128], low)
    T[:, :, 0:128] = mixed.reshape(4, 32, 128)
    T[:, :, 128:256] = top[:, 128:256].reshape(4, 32, 128)
    Tc[...] = enc4(T[...])
    diags = [jnp.sum(jnp.where(ri == ci, g, 0.0), axis=0, keepdims=True) for g in (top[:, 0:128], low)]
    Dg[...] = jnp.where(lax.broadcasted_iota(jnp.int32, (8, 128), 0) == 0, diags[0], diags[1])
    ts = group()
    for k in (2, 1, 3):
        put(Tc.at[(x + k) % 4], Tx.at[k - 1], at_x(k, c), ts)
        put(Dg, Dx.at[k - 1], at_x(k, c), ts)
    wait(ts)
    s = T[x] + dec4(Tx[0]) + dec4(Tx[1]) + dec4(Tx[2])
    Sz[...] = s
    Sc[...] = enc4(s)
    Ds[...] = Dg[...] + Dx[0] + Dx[1] + Dx[2]
    ss = group()
    for k in (2, 1, 3):
        put(Sc, Szr.at[k - 1], at_z(k, c), ss)
        put(Ds, Dz.at[k - 1], at_z(k, c), ss)

    def ungrammed(e, gap, cb):
        centred = e - jnp.mean(e, axis=0, keepdims=True)
        spread = jnp.sqrt(jnp.sum(centred * centred, axis=0, keepdims=True) / (M - 1) + EPS)
        pull = jnp.where(spread < 1.0, -VAR / spread, 0.0)
        diag = jnp.sum(cb * cb, axis=0, keepdims=True) / (M - 1)
        return INV * gap + pull * centred - (COV * diag) * cb

    wait(xswap)
    orows = Xo[...].reshape(M, D_IN)
    for h, wr in enumerate((w, Wo)):
        e, eo = E[h], nn(orows, wr[...])
        cb = Cb[:, h * BLOCK:(h + 1) * BLOCK].astype(F32)
        base[h] = ungrammed(e, e - eo, cb)
        if h == 0:
            cb = (eo - jnp.mean(eo, axis=0, keepdims=True)).astype(BF16)
            Cbo[...] = cb
            base[2] = ungrammed(eo, eo - e, cb.astype(F32))
    XT[0] = rows.T
    XT[1] = orows.T

    wait(ss)
    TA[c, x] = enc4(Sz[...] + dec4(Szr[0]) + dec4(Szr[1]) + dec4(Szr[2]))
    gs, go = group(), group()
    for core, at in ((c, gs), (o, go)):
        for k in (2, 1, 3):
            put(TA.at[c, x], TA.at[c, x], at_x(k, core), at)
    put(TA.at[c, x], TA.at[c, x], partner, go)
    Dt[c] = Ds[...] + Dz[0] + Dz[1] + Dz[2]
    put(Dt.at[c], Dt.at[c], partner, go)
    wait(gs)
    def gram_of(view):
        mixed = dec4(TA[view, :, :, 0:128].reshape(128, 128))
        side = dec4(TA[view, :, :, 128:256].reshape(128, 128))
        flip = mixed.T
        ga = jnp.where(ri == ci, Dt[view, 0:1], jnp.where(ri < ci, mixed, flip))
        gd = jnp.where(ri == ci, Dt[view, 1:2], jnp.where(ri > ci, mixed, flip))
        gram = jnp.concatenate(
            [jnp.concatenate([ga, side], axis=1), jnp.concatenate([side.T, gd], axis=1)], axis=0
        )
        hi = gram.astype(BF16)
        return hi, (gram - hi.astype(F32)).astype(BF16)

    def feature_grad(gram, cb, rest):
        through = nn(gram[0], cb) + nn(gram[1], cb)
        return (rest + through * (COV / (M - 1))).astype(BF16)

    gram = gram_of(c)
    Ff[0] = feature_grad(gram, Cb[:, 0:BLOCK], base[0])
    Ff[1] = feature_grad(gram, Cb[:, BLOCK:2 * BLOCK], base[1])
    part = nn(Ff[0], WT[0]) + nn(Ff[1], WT[1])
    P32[...] = part[:, 0:PCUT].reshape(4, 4, 16, PCUT)
    part = part[:, PCUT:D_IN].reshape(4, 4, 16, PREST)
    halves = (pl.ds(0, PCUT // 2), pl.ds(PCUT // 2, PCUT // 2))
    Pc[...] = enc(P32[...])
    for j in range(4):
        B32[j] = part[:, j]
        Bc[j] = enc(part[:, j])
    L32[...] = nn(XT[0], Ff[0])

    wait(go)
    L32[...] += nn(XT[1], feature_grad(gram_of(o), Cbo[...], base[2]))

    def chunk(q):
        return pl.ds(sum(SIZES[:q]), SIZES[q])

    def rows_of(k, q):
        return pl.ds(pl.multiple_of(((y + k) % 4) * PIECE + sum(SIZES[:q]), 16), SIZES[q])

    direct = {}
    for q in range(CHUNKS):
        direct[q] = group()
        for k in (2, 1, 3):
            Ly[k - 1, chunk(q)] = enc(L32[rows_of(k, q)])
            put(Ly.at[k - 1, chunk(q)], Lr.at[k - 1, chunk(q)], at_y(k), direct[q])
    ps = [group(), group()]
    bz = group()
    for i in range(2):
        for k in (2, 1, 3):
            put(Pc.at[(x + k) % 4, :, :, halves[i]], Px.at[k - 1, :, :, halves[i]], at_x(k, c), ps[i])
        if i == 0:
            for k in (2, 1, 3):
                put(Bc.at[(zh + k) % 4], Bz.at[k - 1], at_z(k, c), bz)
    def at_core(core):
        return pl.ds(pl.multiple_of(core * 8, 8), 8)

    mates = group()

    def sum_a(i):
        wait(ps[i])
        cols = halves[i]
        for j in range(4):
            s = P32[x, j, :, cols] + dec(Px[0, j, :, cols]) + dec(Px[1, j, :, cols]) + dec(Px[2, j, :, cols])
            S32[j, :, cols] = s
            Pz[j, :, cols] = enc(s)
        at = group()
        for k in (2, 1, 3):
            for core in (c, o):
                put(Pz.at[(zh + k) % 4, at_core(core), cols], Pzr.at[k - 1, c, :, cols], at_z(k, core), at)
        put(S32.at[zh, at_core(o), cols], So.at[:, cols], partner, mates)
        return at

    def sum_b():
        wait(bz)
        for j in range(4):
            s = B32[zh, j] + dec(Bz[0, j]) + dec(Bz[1, j]) + dec(Bz[2, j])
            B2[j] = s
            Bx[j] = enc(s)
        at = group()
        for k in (2, 1, 3):
            for core in (c, o):
                put(Bx.at[(x + k) % 4, at_core(core)], Bxr.at[k - 1, c], at_x(k, core), at)
        put(B2.at[x, at_core(o)], Bo, partner, mates)
        return at

    zz, kept = {}, []
    last = group()

    def sum_l(q):
        wait(direct[q])
        at = chunk(q)
        Lz[at] = enc(L32[rows_of(0, q)] + dec(Lr[0, at]) + dec(Lr[1, at]) + dec(Lr[2, at]))
        zz[q] = put(Lz.at[at], Lzr.at[at], across)

    def share_l(q):
        wait(zz[q])
        at = chunk(q)
        La[at] = enc(dec(Lz[at]) + dec(Lzr[at]))
        here = lg.at[rows_of(0, q)]
        for k in (2, 1, 3):
            put(La.at[at], here, at_y(k), last)
        kept.append(pltpu.make_async_copy(La.at[at], here, local.at[q]))
        kept[-1].start()

    pz = []
    sum_l(0)
    sum_l(1)
    pz.append(sum_a(0))
    bs = sum_b()
    share_l(0)
    sum_l(2)
    pz.append(sum_a(1))
    share_l(1)
    sum_l(3)
    share_l(2)
    share_l(3)

    wait(mates)
    mine = at_core(c)

    def total(view, first, second):
        a, b = first, second
        for k in range(3):
            a = a + dec(Pzr[k, view])
            b = b + dec(Bxr[k, view])
        return jnp.concatenate([a, b], axis=1)

    wait(pz[0])
    wait(pz[1])
    wait(bs)
    own = total(c, S32[zh, mine], B2[x, mine])
    other = total(o, So[...], Bo[...])
    first = c == 0
    ig[:, 0, :] = jnp.where(first, own, other)
    ig[:, 1, :] = jnp.where(first, other, own)

    wait(last)
    for copy in kept:
        copy.wait()
    wait(sent)


def finish(ig, lg, image_grad, weight_grad, full, sem):
    copies = [pltpu.make_async_copy(ig, image_grad, sem.at[0])]
    copies[0].start()
    for j in range(5):
        at = pl.ds(j * 256, 256)
        full[at] = dec(lg[at])
        copies.append(pltpu.make_async_copy(full.at[at], weight_grad.at[at], sem.at[1 + j]))
        copies[-1].start()
    for copy in copies:
        copy.wait()


def shards(images, weight):
    V = pltpu.VMEM
    ig, lg = pl.pallas_call(
        kernel,
        out_shape=(
            jax.ShapeDtypeStruct((8, 2, D_IN), F32),
            jax.ShapeDtypeStruct((D_IN, BLOCK), BF16),
        ),
        in_specs=[pl.BlockSpec(memory_space=pltpu.HBM)] * 2,
        out_specs=[pl.BlockSpec(memory_space=V), pl.BlockSpec(memory_space=pl.ANY)],
        scratch_shapes=[
            V((8, 2, D_IN), BF16),
            V((D_IN, BLOCK), BF16),
            V((2, 8, D_IN), BF16),
            V((16, 16, D_IN), BF16),
            V((16, 16, D_IN), BF16),
            V((2, D_IN, M), BF16),
            V((D_IN, BLOCK), BF16),
            V((2, BLOCK, D_IN), BF16),
            V((2, M, BLOCK), F32),
            V((M, 2 * BLOCK), BF16),
            V((M, BLOCK), BF16),
            V((3, M, BLOCK), F32),
            V((4, 32, 256), F32),
            V((4, 32, 256), BF16),
            V((3, 32, 256), BF16),
            V((32, 256), F32),
            V((32, 256), BF16),
            V((3, 32, 256), BF16),
            V((2, 4, 32, 256), BF16),
            V((8, 128), F32),
            V((3, 8, 128), F32),
            V((8, 128), F32),
            V((3, 8, 128), F32),
            V((2, 8, 128), F32),
            V((2, M, BLOCK), BF16),
            V((4, 4, 16, PCUT), F32),
            V((4, 4, 16, PCUT), BF16),
            V((3, 4, 16, PCUT), BF16),
            V((4, 16, PCUT), F32),
            V((4, 16, PCUT), BF16),
            V((3, 2, 8, PCUT), BF16),
            V((8, PCUT), F32),
            V((4, 4, 16, PREST), F32),
            V((4, 4, 16, PREST), BF16),
            V((3, 4, 16, PREST), BF16),
            V((4, 16, PREST), F32),
            V((4, 16, PREST), BF16),
            V((3, 2, 8, PREST), BF16),
            V((8, PREST), F32),
            V((D_IN, BLOCK), F32),
            V((3, PIECE, BLOCK), BF16),
            V((3, PIECE, BLOCK), BF16),
            V((PIECE, BLOCK), BF16),
            V((PIECE, BLOCK), BF16),
            V((PIECE, BLOCK), BF16),
            V((10240, 128), F32),
            pltpu.SemaphoreType.DMA,
            pltpu.SemaphoreType.DMA((NGROUPS,)),
            pltpu.SemaphoreType.DMA((CHUNKS,)),
            pltpu.SemaphoreType.REGULAR,
        ],
        compiler_params=pltpu.CompilerParams(
            collective_id=0, has_side_effects=True, vmem_limit_bytes=VLIM
        ),
    )(pltpu.with_memory_space_constraint(images, pltpu.HBM), pltpu.with_memory_space_constraint(weight, pltpu.HBM))
    return pl.pallas_call(
        finish,
        out_shape=(
            jax.ShapeDtypeStruct((8, 2, D_IN), F32),
            jax.ShapeDtypeStruct((D_IN, BLOCK), F32),
        ),
        in_specs=[pl.BlockSpec(memory_space=V)] * 2,
        out_specs=[pl.BlockSpec(memory_space=pl.ANY)] * 2,
        scratch_shapes=[V((D_IN, BLOCK), F32), pltpu.SemaphoreType.DMA((6,))],
        compiler_params=pltpu.CompilerParams(vmem_limit_bytes=4 * 2**20),
    )(ig, lg)


NGROUPS = 26 + CHUNKS
VLIM = 24 * 2**20


def solution(mesh):
    return jax.shard_map(
        shards,
        mesh=mesh,
        in_specs=(P(("rep", "dp"), None, None), P(None, "dp")),
        out_specs=(P(("rep", "dp"), None, None), P(None, "dp")),
        check_vma=False,
    )
```

```python
import jax
import jax.numpy as jnp
from jax import lax
from jax.experimental import pallas as pl
from jax.experimental.pallas import tpu as pltpu
from jax.sharding import PartitionSpec as P

MESH = pl.DeviceIdType.MESH
F32, BF16 = jnp.float32, jnp.bfloat16

N_REP, N_DP = 8, 32
M = 256
D_IN = 1280
BLOCK = 256
EMB = BLOCK * N_DP
S = 8192.0 / N_REP
EPS = 0.0001
INV = S * 2.0 * 25.0 / (M * EMB)
VAR = S * 25.0 / (EMB * (M - 1))
COV = S * 4.0 / (EMB * (M - 1))
PIECE = D_IN // 4
SIZES = (64, 96, 96)
LATE = sum(SIZES)
ZROWS = PIECE - LATE
CHUNKS = len(SIZES)
CUT = 896
REST = D_IN - CUT
PCUT = 1024
PREST = D_IN - PCUT
GRAM_UNIT = 2.0**-10


def root(t):
    return jnp.sqrt(jnp.abs(t))


def enc(v):
    return (v * jnp.abs(v)).astype(BF16)


def dec(b):
    t = b.astype(F32)
    s = root(t)
    return jnp.where(t < 0.0, -s, s)


def enc4(g):
    v = g * GRAM_UNIT
    return ((v * jnp.abs(v)) * (v * v)).astype(BF16)


def dec4(b):
    t = b.astype(F32)
    s = root(root(t)) * (1.0 / GRAM_UNIT)
    return jnp.where(t < 0.0, -s, s)


def nt(a, b):
    return lax.dot_general(a, b, (((1,), (1,)), ((), ())), preferred_element_type=F32)


def tn(a, b):
    return lax.dot_general(a, b, (((0,), (0,)), ((), ())), preferred_element_type=F32)


def nn(a, b):
    return jnp.dot(a, b, preferred_element_type=F32)


class Group:
    def __init__(self, sem):
        self.sem, self.kib = sem, 0


def kernel(
    img, w_hbm, ig, lg,
    Iv, w, I2, X, Xo, XT, Wo, WT, E, Cb, Cbo, base,
    T, Tc, Tx, Sz, Sc, Szr, TA, Dg, Dx, Ds, Dz, Dt,
    Ff,
    P32, Pc, Px, S32, Pz, Pzr, So,
    B32, Bc, Bz, B2, Bx, Bxr, Bo,
    L32, Ly, Lr, Lz, Lzr, La,
    Zc, Zr, H, Hc, Hr, Ht,
    span, send, recv, local, near,
):
    rep, dp = lax.axis_index("rep"), lax.axis_index("dp")
    y, zl = rep // 2, rep % 2
    c, chip = dp % 2, dp // 2
    x, zh = chip // 4, chip % 4
    o = 1 - c

    partner = (rep, chip * 2 + o)

    def at_x(k, core):
        return (rep, (((x + k) % 4) * 4 + zh) * 2 + core)

    def at_z(k, core):
        return (rep, (x * 4 + (zh + k) % 4) * 2 + core)

    def at_y(k):
        return (((y + k) % 4) * 2 + zl, dp)

    across = (y * 2 + (1 - zl), dp)

    fetch = pltpu.make_async_copy(img, Iv, local.at[0])
    fetch.start()
    wfetch = pltpu.make_async_copy(w_hbm, w, local.at[1])
    wfetch.start()
    barrier = pltpu.get_barrier_semaphore()
    peers = [partner, across]
    for k in (1, 2, 3):
        peers += [at_x(k, c), at_x(k, o), at_y(k)]
    for k in (1, 3):
        peers += [at_z(k, c), at_z(k, o)]
    for peer in peers:
        pl.semaphore_signal(barrier, inc=1, device_id=peer, device_id_type=MESH)
    fetch.wait()
    both = Iv[...].astype(F32)
    I2[0] = both[:, 0, :].astype(BF16)
    I2[1] = both[:, 1, :].astype(BF16)
    pl.semaphore_wait(barrier, len(peers))
    pl.semaphore_signal(near, inc=1, device_id=at_z(1, c), device_id_type=MESH)

    sent = Group(send)
    groups = []

    def group():
        groups.append(Group(recv.at[len(groups)]))
        return groups[-1]

    def put(src, dst, device, at=None):
        at = at or group()
        copy = pltpu.make_async_remote_copy(
            src_ref=src, dst_ref=dst, send_sem=sent.sem, recv_sem=at.sem,
            device_id=device, device_id_type=MESH,
        )
        copy.start()
        size = 1
        for n in src.shape:
            size *= n
        kib = size * jnp.dtype(src.dtype).itemsize // 1024
        at.kib += kib
        sent.kib += kib
        return at

    def wait(at):
        part = span.at[pl.ds(0, at.kib * 2)]
        pltpu.make_async_copy(part, part, at.sem).wait()

    at = pl.ds(pl.multiple_of(c * 8, 8), 8)
    A, B = pl.ds(0, CUT), pl.ds(CUT, REST)
    az, bx = {}, {}
    for k in (1, 3, 2):
        az[k], bx[k] = group(), group()
        for core in (c, o):
            if k != 2:
                put(I2.at[core, :, A], X.at[chip, at, A], at_z(k, core), az[k])
            put(I2.at[core, :, B], X.at[chip, at, B], at_x(k, core), bx[k])
    mate = put(I2.at[o], X.at[chip, at], partner)
    keep = pltpu.make_async_copy(I2.at[c], X.at[chip, at], local.at[0])
    keep.start()
    wswap = put(w_hbm, Wo, partner)
    keep.wait()
    wait(mate)
    forwards = group()
    pl.semaphore_wait(near, 1)
    for core in (c, o):
        put(I2.at[core, :, A], X.at[chip, at, A], at_z(2, core), az[2])
    for name, k in (("A", 0), ("B", 0), ("B", 1), ("B", 3), ("A", 1), ("A", 3), ("B", 2), ("A", 2)):
        if name == "A":
            if k:
                wait(az[k])
            slot = x * 4 + (zh - k + 4) % 4
            for j in (2, 1, 3):
                put(X.at[slot, :, A], X.at[slot, :, A], at_x(j, c), forwards)
        else:
            if k:
                wait(bx[k])
            slot = ((x - k + 4) % 4) * 4 + zh
            for j in (2, 1, 3):
                put(X.at[slot, :, B], X.at[slot, :, B], at_z(j, c), forwards)
    wait(wswap)
    wfetch.wait()
    WT[0] = w[...].T
    WT[1] = Wo[...].T
    wait(forwards)
    xswap = put(X, Xo, partner)

    rows = X[...].reshape(M, D_IN)
    for h, wr in enumerate((w, Wo)):
        e = nn(rows, wr[...])
        E[h] = e
        Cb[:, h * BLOCK:(h + 1) * BLOCK] = (e - jnp.mean(e, axis=0, keepdims=True)).astype(BF16)
    ri = lax.broadcasted_iota(jnp.int32, (128, 128), 0)
    ci = lax.broadcasted_iota(jnp.int32, (128, 128), 1)
    top = nt(Cb[0:128, :], Cb[...])
    low = nt(Cb[128:256, :], Cb[128:256, :])
    mixed = jnp.where(ri <= ci, top[:, 0:128], low)
    T[:, :, 0:128] = mixed.reshape(4, 32, 128)
    T[:, :, 128:256] = top[:, 128:256].reshape(4, 32, 128)
    Tc[...] = enc4(T[...])
    diags = [jnp.sum(jnp.where(ri == ci, g, 0.0), axis=0, keepdims=True) for g in (top[:, 0:128], low)]
    Dg[...] = jnp.where(lax.broadcasted_iota(jnp.int32, (8, 128), 0) == 0, diags[0], diags[1])
    ts = group()
    for k in (2, 1, 3):
        put(Tc.at[(x + k) % 4], Tx.at[k - 1], at_x(k, c), ts)
        put(Dg, Dx.at[k - 1], at_x(k, c), ts)
    wait(ts)
    s = T[x] + dec4(Tx[0]) + dec4(Tx[1]) + dec4(Tx[2])
    Sz[...] = s
    Sc[...] = enc4(s)
    Ds[...] = Dg[...] + Dx[0] + Dx[1] + Dx[2]
    ss = group()
    for k in (2, 1, 3):
        put(Sc, Szr.at[k - 1], at_z(k, c), ss)
        put(Ds, Dz.at[k - 1], at_z(k, c), ss)

    def ungrammed(e, gap, cb):
        centred = e - jnp.mean(e, axis=0, keepdims=True)
        spread = jnp.sqrt(jnp.sum(centred * centred, axis=0, keepdims=True) / (M - 1) + EPS)
        pull = jnp.where(spread < 1.0, -VAR / spread, 0.0)
        diag = jnp.sum(cb * cb, axis=0, keepdims=True) / (M - 1)
        return INV * gap + pull * centred - (COV * diag) * cb

    wait(xswap)
    orows = Xo[...].reshape(M, D_IN)
    for h, wr in enumerate((w, Wo)):
        e, eo = E[h], nn(orows, wr[...])
        cb = Cb[:, h * BLOCK:(h + 1) * BLOCK].astype(F32)
        base[h] = ungrammed(e, e - eo, cb)
        if h == 0:
            cb = (eo - jnp.mean(eo, axis=0, keepdims=True)).astype(BF16)
            Cbo[...] = cb
            base[2] = ungrammed(eo, eo - e, cb.astype(F32))
    XT[0] = rows.T
    XT[1] = orows.T

    wait(ss)
    TA[c, x] = enc4(Sz[...] + dec4(Szr[0]) + dec4(Szr[1]) + dec4(Szr[2]))
    gs, go = group(), group()
    for core, at in ((c, gs), (o, go)):
        for k in (2, 1, 3):
            put(TA.at[c, x], TA.at[c, x], at_x(k, core), at)
    put(TA.at[c, x], TA.at[c, x], partner, go)
    Dt[c] = Ds[...] + Dz[0] + Dz[1] + Dz[2]
    put(Dt.at[c], Dt.at[c], partner, go)
    wait(gs)
    def gram_of(view):
        mixed = dec4(TA[view, :, :, 0:128].reshape(128, 128))
        side = dec4(TA[view, :, :, 128:256].reshape(128, 128))
        flip = mixed.T
        ga = jnp.where(ri == ci, Dt[view, 0:1], jnp.where(ri < ci, mixed, flip))
        gd = jnp.where(ri == ci, Dt[view, 1:2], jnp.where(ri > ci, mixed, flip))
        gram = jnp.concatenate(
            [jnp.concatenate([ga, side], axis=1), jnp.concatenate([side.T, gd], axis=1)], axis=0
        )
        hi = gram.astype(BF16)
        return hi, (gram - hi.astype(F32)).astype(BF16)

    def feature_grad(gram, cb, rest):
        through = nn(gram[0], cb) + nn(gram[1], cb)
        return (rest + through * (COV / (M - 1))).astype(BF16)

    gram = gram_of(c)
    Ff[0] = feature_grad(gram, Cb[:, 0:BLOCK], base[0])
    Ff[1] = feature_grad(gram, Cb[:, BLOCK:2 * BLOCK], base[1])
    part = nn(Ff[0], WT[0]) + nn(Ff[1], WT[1])
    P32[...] = part[:, 0:PCUT].reshape(4, 4, 16, PCUT)
    part = part[:, PCUT:D_IN].reshape(4, 4, 16, PREST)
    halves = (pl.ds(0, PCUT // 2), pl.ds(PCUT // 2, PCUT // 2))
    Pc[...] = enc(P32[...])
    for j in range(4):
        B32[j] = part[:, j]
        Bc[j] = enc(part[:, j])
    L32[...] = nn(XT[0], Ff[0])

    wait(go)
    L32[...] += nn(XT[1], feature_grad(gram_of(o), Cbo[...], base[2]))

    def chunk(q):
        return pl.ds(sum(SIZES[:q]), SIZES[q])

    def rows_of(k, q):
        return pl.ds(pl.multiple_of(((y + k) % 4) * PIECE + sum(SIZES[:q]), 16), SIZES[q])

    def z_rows(piece):
        return pl.ds(pl.multiple_of(piece * PIECE + LATE, 16), ZROWS)

    mine_z = pl.ds(pl.multiple_of(zl * 128, 128), 128)
    other_z = pl.ds(pl.multiple_of((1 - zl) * 128, 128), 128)
    for p in range(4):
        Zc[p] = enc(L32[z_rows(p), other_z])
    za = put(Zc, Zr, across)
    direct = {}
    for q in range(CHUNKS):
        direct[q] = group()
        for k in (2, 1, 3):
            Ly[k - 1, chunk(q)] = enc(L32[rows_of(k, q)])
            put(Ly.at[k - 1, chunk(q)], Lr.at[k - 1, chunk(q)], at_y(k), direct[q])
    ps = [group(), group()]
    bz = group()
    for i in range(2):
        for k in (2, 1, 3):
            put(Pc.at[(x + k) % 4, :, :, halves[i]], Px.at[k - 1, :, :, halves[i]], at_x(k, c), ps[i])
        if i == 0:
            for k in (2, 1, 3):
                put(Bc.at[(zh + k) % 4], Bz.at[k - 1], at_z(k, c), bz)
    def at_core(core):
        return pl.ds(pl.multiple_of(core * 8, 8), 8)

    mates = group()

    def sum_a(i):
        wait(ps[i])
        cols = halves[i]
        for j in range(4):
            s = P32[x, j, :, cols] + dec(Px[0, j, :, cols]) + dec(Px[1, j, :, cols]) + dec(Px[2, j, :, cols])
            S32[j, :, cols] = s
            Pz[j, :, cols] = enc(s)
        at = group()
        for k in (2, 1, 3):
            for core in (c, o):
                put(Pz.at[(zh + k) % 4, at_core(core), cols], Pzr.at[k - 1, c, :, cols], at_z(k, core), at)
        put(S32.at[zh, at_core(o), cols], So.at[:, cols], partner, mates)
        return at

    def sum_b():
        wait(bz)
        for j in range(4):
            s = B32[zh, j] + dec(Bz[0, j]) + dec(Bz[1, j]) + dec(Bz[2, j])
            B2[j] = s
            Bx[j] = enc(s)
        at = group()
        for k in (2, 1, 3):
            for core in (c, o):
                put(Bx.at[(x + k) % 4, at_core(core)], Bxr.at[k - 1, c], at_x(k, core), at)
        put(B2.at[x, at_core(o)], Bo, partner, mates)
        return at

    zz, kept = {}, []
    last = group()

    def sum_l(q):
        wait(direct[q])
        at = chunk(q)
        Lz[at] = enc(L32[rows_of(0, q)] + dec(Lr[0, at]) + dec(Lr[1, at]) + dec(Lr[2, at]))
        zz[q] = put(Lz.at[at], Lzr.at[at], across)

    def share_l(q):
        wait(zz[q])
        at = chunk(q)
        La[at] = enc(dec(Lz[at]) + dec(Lzr[at]))
        here = lg.at[rows_of(0, q)]
        for k in (2, 1, 3):
            put(La.at[at], here, at_y(k), last)
        kept.append(pltpu.make_async_copy(La.at[at], here, local.at[q]))
        kept[-1].start()

    zw = group()
    zy = group()
    zlast = group()

    def z_first():
        wait(za)
        for p in range(4):
            H[p] = L32[z_rows(p), mine_z] + dec(Zr[p])
        for k in (2, 1, 3):
            Hc[k - 1] = enc(H[(y + k) % 4])
            put(Hc.at[k - 1], Hr.at[k - 1], at_y(k), zw)

    def z_second():
        wait(zw)
        Ht[...] = enc(H[y] + dec(Hr[0]) + dec(Hr[1]) + dec(Hr[2]))
        here = lg.at[z_rows(y), mine_z]
        for k in (2, 1, 3):
            put(Ht, here, at_y(k), zy)
        put(Ht, here, across, zlast)
        kept.append(pltpu.make_async_copy(Ht, here, local.at[CHUNKS]))
        kept[-1].start()

    def z_third():
        wait(zy)
        for k in (1, 2, 3):
            there = lg.at[z_rows((y + k) % 4), mine_z]
            put(there, there, across, zlast)

    pz = []
    z_first()
    sum_l(0)
    sum_l(1)
    pz.append(sum_a(0))
    bs = sum_b()
    share_l(0)
    sum_l(2)
    pz.append(sum_a(1))
    z_second()
    share_l(1)
    share_l(2)
    z_third()

    wait(mates)
    mine = at_core(c)

    def total(view, first, second):
        a, b = first, second
        for k in range(3):
            a = a + dec(Pzr[k, view])
            b = b + dec(Bxr[k, view])
        return jnp.concatenate([a, b], axis=1)

    wait(pz[0])
    wait(pz[1])
    wait(bs)
    own = total(c, S32[zh, mine], B2[x, mine])
    other = total(o, So[...], Bo[...])
    first = c == 0
    ig[:, 0, :] = jnp.where(first, own, other)
    ig[:, 1, :] = jnp.where(first, other, own)

    wait(last)
    wait(zlast)
    for copy in kept:
        copy.wait()
    wait(sent)


def finish(ig, lg, image_grad, weight_grad, full, sem):
    copies = [pltpu.make_async_copy(ig, image_grad, sem.at[0])]
    copies[0].start()
    for j in range(5):
        at = pl.ds(j * 256, 256)
        full[at] = dec(lg[at])
        copies.append(pltpu.make_async_copy(full.at[at], weight_grad.at[at], sem.at[1 + j]))
        copies[-1].start()
    for copy in copies:
        copy.wait()


def shards(images, weight):
    V = pltpu.VMEM
    ig, lg = pl.pallas_call(
        kernel,
        out_shape=(
            jax.ShapeDtypeStruct((8, 2, D_IN), F32),
            jax.ShapeDtypeStruct((D_IN, BLOCK), BF16),
        ),
        in_specs=[pl.BlockSpec(memory_space=pltpu.HBM)] * 2,
        out_specs=[pl.BlockSpec(memory_space=V), pl.BlockSpec(memory_space=pl.ANY)],
        scratch_shapes=[
            V((8, 2, D_IN), BF16),
            V((D_IN, BLOCK), BF16),
            V((2, 8, D_IN), BF16),
            V((16, 16, D_IN), BF16),
            V((16, 16, D_IN), BF16),
            V((2, D_IN, M), BF16),
            V((D_IN, BLOCK), BF16),
            V((2, BLOCK, D_IN), BF16),
            V((2, M, BLOCK), F32),
            V((M, 2 * BLOCK), BF16),
            V((M, BLOCK), BF16),
            V((3, M, BLOCK), F32),
            V((4, 32, 256), F32),
            V((4, 32, 256), BF16),
            V((3, 32, 256), BF16),
            V((32, 256), F32),
            V((32, 256), BF16),
            V((3, 32, 256), BF16),
            V((2, 4, 32, 256), BF16),
            V((8, 128), F32),
            V((3, 8, 128), F32),
            V((8, 128), F32),
            V((3, 8, 128), F32),
            V((2, 8, 128), F32),
            V((2, M, BLOCK), BF16),
            V((4, 4, 16, PCUT), F32),
            V((4, 4, 16, PCUT), BF16),
            V((3, 4, 16, PCUT), BF16),
            V((4, 16, PCUT), F32),
            V((4, 16, PCUT), BF16),
            V((3, 2, 8, PCUT), BF16),
            V((8, PCUT), F32),
            V((4, 4, 16, PREST), F32),
            V((4, 4, 16, PREST), BF16),
            V((3, 4, 16, PREST), BF16),
            V((4, 16, PREST), F32),
            V((4, 16, PREST), BF16),
            V((3, 2, 8, PREST), BF16),
            V((8, PREST), F32),
            V((D_IN, BLOCK), F32),
            V((3, LATE, BLOCK), BF16),
            V((3, LATE, BLOCK), BF16),
            V((LATE, BLOCK), BF16),
            V((LATE, BLOCK), BF16),
            V((LATE, BLOCK), BF16),
            V((4, ZROWS, 128), BF16),
            V((4, ZROWS, 128), BF16),
            V((4, ZROWS, 128), F32),
            V((3, ZROWS, 128), BF16),
            V((3, ZROWS, 128), BF16),
            V((ZROWS, 128), BF16),
            V((10240, 128), F32),
            pltpu.SemaphoreType.DMA,
            pltpu.SemaphoreType.DMA((NGROUPS,)),
            pltpu.SemaphoreType.DMA((CHUNKS + 1,)),
            pltpu.SemaphoreType.REGULAR,
        ],
        compiler_params=pltpu.CompilerParams(
            collective_id=0, has_side_effects=True, vmem_limit_bytes=VLIM
        ),
    )(pltpu.with_memory_space_constraint(images, pltpu.HBM), pltpu.with_memory_space_constraint(weight, pltpu.HBM))
    return pl.pallas_call(
        finish,
        out_shape=(
            jax.ShapeDtypeStruct((8, 2, D_IN), F32),
            jax.ShapeDtypeStruct((D_IN, BLOCK), F32),
        ),
        in_specs=[pl.BlockSpec(memory_space=V)] * 2,
        out_specs=[pl.BlockSpec(memory_space=pl.ANY)] * 2,
        scratch_shapes=[V((D_IN, BLOCK), F32), pltpu.SemaphoreType.DMA((6,))],
        compiler_params=pltpu.CompilerParams(vmem_limit_bytes=4 * 2**20),
    )(ig, lg)


NGROUPS = 30 + CHUNKS
VLIM = 24 * 2**20


def solution(mesh):
    return jax.shard_map(
        shards,
        mesh=mesh,
        in_specs=(P(("rep", "dp"), None, None), P(None, "dp")),
        out_specs=(P(("rep", "dp"), None, None), P(None, "dp")),
        check_vma=False,
    )
```

```python
import jax
import jax.numpy as jnp
from jax import lax
from jax.experimental import pallas as pl
from jax.experimental.pallas import tpu as pltpu
from jax.sharding import PartitionSpec as P

MESH = pl.DeviceIdType.MESH
F32, BF16 = jnp.float32, jnp.bfloat16

N_REP, N_DP = 8, 32
M = 256
D_IN = 1280
BLOCK = 256
EMB = BLOCK * N_DP
S = 8192.0 / N_REP
EPS = 0.0001
INV = S * 2.0 * 25.0 / (M * EMB)
VAR = S * 25.0 / (EMB * (M - 1))
COV = S * 4.0 / (EMB * (M - 1))
PIECE = D_IN // 4
SIZES = (64, 96, 96)
LATE = sum(SIZES)
ZROWS = PIECE - LATE
CHUNKS = len(SIZES)
CUT = 1024
REST = D_IN - CUT
PCUT = 1024
PREST = D_IN - PCUT
GRAM_UNIT = 2.0**-10


def root(t):
    return jnp.sqrt(jnp.abs(t))


def enc(v):
    return (v * jnp.abs(v)).astype(BF16)


def dec(b):
    t = b.astype(F32)
    s = root(t)
    return jnp.where(t < 0.0, -s, s)


def enc4(g):
    v = g * GRAM_UNIT
    return ((v * jnp.abs(v)) * (v * v)).astype(BF16)


def dec4(b):
    t = b.astype(F32)
    s = root(root(t)) * (1.0 / GRAM_UNIT)
    return jnp.where(t < 0.0, -s, s)


def nt(a, b):
    return lax.dot_general(a, b, (((1,), (1,)), ((), ())), preferred_element_type=F32)


def tn(a, b):
    return lax.dot_general(a, b, (((0,), (0,)), ((), ())), preferred_element_type=F32)


def nn(a, b):
    return jnp.dot(a, b, preferred_element_type=F32)


class Group:
    def __init__(self, sem):
        self.sem, self.kib = sem, 0


def kernel(
    img, w_hbm, ig, lg,
    Iv, w, I2, X, Xo, XT, Wo, WT, E, Cb, Cbo, base,
    T, Tc, Tx, Sz, Sc, Szr, TA, Dg, Dx, Ds, Dz, Dt,
    Ff,
    P32, Pc, Px, S32, Pz, Pzr, So,
    B32, Bc, Bz, B2, Bx, Bxr, Bo,
    L32, Ly, Lr, Lz, Lzr, La,
    Zc, Zr, H, Hc, Hr, Ht,
    span, send, recv, local, near,
):
    rep, dp = lax.axis_index("rep"), lax.axis_index("dp")
    y, zl = rep // 2, rep % 2
    c, chip = dp % 2, dp // 2
    x, zh = chip // 4, chip % 4
    o = 1 - c

    partner = (rep, chip * 2 + o)

    def at_x(k, core):
        return (rep, (((x + k) % 4) * 4 + zh) * 2 + core)

    def at_z(k, core):
        return (rep, (x * 4 + (zh + k) % 4) * 2 + core)

    def at_y(k):
        return (((y + k) % 4) * 2 + zl, dp)

    across = (y * 2 + (1 - zl), dp)

    fetch = pltpu.make_async_copy(img, Iv, local.at[0])
    fetch.start()
    wfetch = pltpu.make_async_copy(w_hbm, w, local.at[1])
    wfetch.start()
    barrier = pltpu.get_barrier_semaphore()
    peers = [at_z(k, core) for k in (1, 3) for core in (c, o)]
    for k in (2, 1, 3):
        peers += [at_x(k, c), at_x(k, o), at_y(k)]
    peers += [across, partner]
    for peer in peers:
        pl.semaphore_signal(barrier, inc=1, device_id=peer, device_id_type=MESH)
    fetch.wait()
    both = Iv[...].astype(F32)
    I2[0] = both[:, 0, :].astype(BF16)
    I2[1] = both[:, 1, :].astype(BF16)
    pl.semaphore_wait(barrier, len(peers))
    pl.semaphore_signal(near, inc=1, device_id=at_z(1, c), device_id_type=MESH)

    sent = Group(send)
    groups = []

    def group():
        groups.append(Group(recv.at[len(groups)]))
        return groups[-1]

    def put(src, dst, device, at=None):
        at = at or group()
        copy = pltpu.make_async_remote_copy(
            src_ref=src, dst_ref=dst, send_sem=sent.sem, recv_sem=at.sem,
            device_id=device, device_id_type=MESH,
        )
        copy.start()
        size = 1
        for n in src.shape:
            size *= n
        kib = size * jnp.dtype(src.dtype).itemsize // 1024
        at.kib += kib
        sent.kib += kib
        return at

    def wait(at):
        part = span.at[pl.ds(0, at.kib * 2)]
        pltpu.make_async_copy(part, part, at.sem).wait()

    at = pl.ds(pl.multiple_of(c * 8, 8), 8)
    A, B = pl.ds(0, CUT), pl.ds(CUT, REST)
    az, bx = {}, {}
    for k in (1, 3, 2):
        az[k], bx[k] = group(), group()
        for core in (c, o):
            if k != 2:
                put(I2.at[core, :, A], X.at[chip, at, A], at_z(k, core), az[k])
            put(I2.at[core, :, B], X.at[chip, at, B], at_x(k, core), bx[k])
    mate = put(I2.at[o], X.at[chip, at], partner)
    keep = pltpu.make_async_copy(I2.at[c], X.at[chip, at], local.at[0])
    keep.start()
    wswap = put(w_hbm, Wo, partner)
    keep.wait()
    wait(mate)
    forwards = group()
    pl.semaphore_wait(near, 1)
    for core in (c, o):
        put(I2.at[core, :, A], X.at[chip, at, A], at_z(2, core), az[2])
    for name, k in (("A", 0), ("A", 1), ("A", 3), ("B", 0), ("B", 1), ("B", 3), ("B", 2), ("A", 2)):
        if name == "A":
            if k:
                wait(az[k])
            slot = x * 4 + (zh - k + 4) % 4
            for j in (2, 1, 3):
                put(X.at[slot, :, A], X.at[slot, :, A], at_x(j, c), forwards)
        else:
            if k:
                wait(bx[k])
            slot = ((x - k + 4) % 4) * 4 + zh
            for j in (2, 1, 3):
                put(X.at[slot, :, B], X.at[slot, :, B], at_z(j, c), forwards)
    wait(wswap)
    wfetch.wait()
    WT[0:BLOCK] = w[...].T
    WT[BLOCK:2 * BLOCK] = Wo[...].T
    wait(forwards)
    xswap = put(X, Xo, partner)

    rows = X[...].reshape(M, D_IN)
    for h, wr in enumerate((w, Wo)):
        e = nn(rows, wr[...])
        E[h] = e
        Cb[:, h * BLOCK:(h + 1) * BLOCK] = (e - jnp.mean(e, axis=0, keepdims=True)).astype(BF16)
    ri = lax.broadcasted_iota(jnp.int32, (128, 128), 0)
    ci = lax.broadcasted_iota(jnp.int32, (128, 128), 1)
    top = nt(Cb[0:128, :], Cb[...])
    low = nt(Cb[128:256, :], Cb[128:256, :])
    mixed = jnp.where(ri <= ci, top[:, 0:128], low)
    T[:, :, 0:128] = mixed.reshape(4, 32, 128)
    T[:, :, 128:256] = top[:, 128:256].reshape(4, 32, 128)
    Tc[...] = enc4(T[...])
    diags = [jnp.sum(jnp.where(ri == ci, g, 0.0), axis=0, keepdims=True) for g in (top[:, 0:128], low)]
    Dg[...] = jnp.where(lax.broadcasted_iota(jnp.int32, (8, 128), 0) == 0, diags[0], diags[1])
    ts = group()
    for k in (2, 1, 3):
        put(Tc.at[(x + k) % 4], Tx.at[k - 1], at_x(k, c), ts)
        put(Dg, Dx.at[k - 1], at_x(k, c), ts)
    wait(ts)
    s = T[x] + dec4(Tx[0]) + dec4(Tx[1]) + dec4(Tx[2])
    Sz[...] = s
    Sc[...] = enc4(s)
    Ds[...] = Dg[...] + Dx[0] + Dx[1] + Dx[2]
    ss = group()
    for k in (2, 1, 3):
        put(Sc, Szr.at[k - 1], at_z(k, c), ss)
        put(Ds, Dz.at[k - 1], at_z(k, c), ss)

    def ungrammed(e, gap, cb):
        centred = e - jnp.mean(e, axis=0, keepdims=True)
        spread = jnp.sqrt(jnp.sum(centred * centred, axis=0, keepdims=True) / (M - 1) + EPS)
        pull = jnp.where(spread < 1.0, -VAR / spread, 0.0)
        diag = jnp.sum(cb * cb, axis=0, keepdims=True) / (M - 1)
        return INV * gap + pull * centred - (COV * diag) * cb

    wait(xswap)
    orows = Xo[...].reshape(M, D_IN)
    for h, wr in enumerate((w, Wo)):
        e, eo = E[h], nn(orows, wr[...])
        cb = Cb[:, h * BLOCK:(h + 1) * BLOCK].astype(F32)
        base[h] = ungrammed(e, e - eo, cb)
        if h == 0:
            cb = (eo - jnp.mean(eo, axis=0, keepdims=True)).astype(BF16)
            Cbo[...] = cb
            base[2] = ungrammed(eo, eo - e, cb.astype(F32))
    XT[0] = rows.T
    XT[1] = orows.T

    wait(ss)
    TA[c, x] = enc4(Sz[...] + dec4(Szr[0]) + dec4(Szr[1]) + dec4(Szr[2]))
    gs, go = group(), group()
    for core, at in ((c, gs), (o, go)):
        for k in (2, 1, 3):
            put(TA.at[c, x], TA.at[c, x], at_x(k, core), at)
    put(TA.at[c, x], TA.at[c, x], partner, go)
    Dt[c] = Ds[...] + Dz[0] + Dz[1] + Dz[2]
    put(Dt.at[c], Dt.at[c], partner, go)
    wait(gs)
    def gram_of(view):
        mixed = dec4(TA[view, :, :, 0:128].reshape(128, 128))
        side = dec4(TA[view, :, :, 128:256].reshape(128, 128))
        flip = mixed.T
        ga = jnp.where(ri == ci, Dt[view, 0:1], jnp.where(ri < ci, mixed, flip))
        gd = jnp.where(ri == ci, Dt[view, 1:2], jnp.where(ri > ci, mixed, flip))
        gram = jnp.concatenate(
            [jnp.concatenate([ga, side], axis=1), jnp.concatenate([side.T, gd], axis=1)], axis=0
        )
        hi = gram.astype(BF16)
        return hi, (gram - hi.astype(F32)).astype(BF16)

    def feature_grad(gram, cb, rest):
        through = nn(gram[0], cb) + nn(gram[1], cb)
        return (rest + through * (COV / (M - 1))).astype(BF16)

    gram = gram_of(c)
    Ff[:, 0:BLOCK] = feature_grad(gram, Cb[:, 0:BLOCK], base[0])
    Ff[:, BLOCK:2 * BLOCK] = feature_grad(gram, Cb[:, BLOCK:2 * BLOCK], base[1])
    part = nn(Ff[...], WT[...])
    main = part[:, 0:PCUT].reshape(4, 4, 16, PCUT)
    P32[...] = main
    Pc[...] = enc(main)
    part = part[:, PCUT:D_IN].reshape(4, 4, 16, PREST)
    halves = (pl.ds(0, PCUT // 2), pl.ds(PCUT // 2, PCUT // 2))
    for j in range(4):
        B32[j] = part[:, j]
        Bc[j] = enc(part[:, j])
    L32[...] = nn(XT[0], Ff[:, 0:BLOCK])

    wait(go)
    L32[...] += nn(XT[1], feature_grad(gram_of(o), Cbo[...], base[2]))

    def chunk(q):
        return pl.ds(sum(SIZES[:q]), SIZES[q])

    def rows_of(k, q):
        return pl.ds(pl.multiple_of(((y + k) % 4) * PIECE + sum(SIZES[:q]), 16), SIZES[q])

    def z_rows(piece):
        return pl.ds(pl.multiple_of(piece * PIECE + LATE, 16), ZROWS)

    mine_z = pl.ds(pl.multiple_of(zl * 128, 128), 128)
    other_z = pl.ds(pl.multiple_of((1 - zl) * 128, 128), 128)
    for p in range(4):
        Zc[p] = enc(L32[z_rows(p), other_z])
    za = put(Zc, Zr, across)
    direct = {}
    for q in range(CHUNKS):
        direct[q] = group()
        for k in (2, 1, 3):
            Ly[k - 1, chunk(q)] = enc(L32[rows_of(k, q)])
            put(Ly.at[k - 1, chunk(q)], Lr.at[k - 1, chunk(q)], at_y(k), direct[q])
    ps = [group(), group()]
    bz = group()
    for i in range(2):
        for k in (2, 1, 3):
            put(Pc.at[(x + k) % 4, :, :, halves[i]], Px.at[k - 1, :, :, halves[i]], at_x(k, c), ps[i])
        if i == 0:
            for k in (2, 1, 3):
                put(Bc.at[(zh + k) % 4], Bz.at[k - 1], at_z(k, c), bz)
    def at_core(core):
        return pl.ds(pl.multiple_of(core * 8, 8), 8)

    mates = group()

    def sum_a(i):
        wait(ps[i])
        cols = halves[i]
        for j in range(4):
            s = P32[x, j, :, cols] + dec(Px[0, j, :, cols]) + dec(Px[1, j, :, cols]) + dec(Px[2, j, :, cols])
            S32[j, :, cols] = s
            Pz[j, :, cols] = enc(s)
        at = group()
        for k in (2, 1, 3):
            for core in (c, o):
                put(Pz.at[(zh + k) % 4, at_core(core), cols], Pzr.at[k - 1, c, :, cols], at_z(k, core), at)
        put(S32.at[zh, at_core(o), cols], So.at[:, cols], partner, mates)
        return at

    def sum_b():
        wait(bz)
        for j in range(4):
            s = B32[zh, j] + dec(Bz[0, j]) + dec(Bz[1, j]) + dec(Bz[2, j])
            B2[j] = s
            Bx[j] = enc(s)
        at = group()
        for k in (2, 1, 3):
            for core in (c, o):
                put(Bx.at[(x + k) % 4, at_core(core)], Bxr.at[k - 1, c], at_x(k, core), at)
        put(B2.at[x, at_core(o)], Bo, partner, mates)
        return at

    zz, kept = {}, []
    last = group()

    def sum_l(q):
        wait(direct[q])
        at = chunk(q)
        Lz[at] = enc(L32[rows_of(0, q)] + dec(Lr[0, at]) + dec(Lr[1, at]) + dec(Lr[2, at]))
        zz[q] = put(Lz.at[at], Lzr.at[at], across)

    def share_l(q):
        wait(zz[q])
        at = chunk(q)
        La[at] = enc(dec(Lz[at]) + dec(Lzr[at]))
        here = lg.at[rows_of(0, q)]
        for k in (2, 1, 3):
            put(La.at[at], here, at_y(k), last)
        kept.append(pltpu.make_async_copy(La.at[at], here, local.at[q]))
        kept[-1].start()

    zw = group()
    zy = group()
    zlast = group()

    def z_first():
        wait(za)
        for p in range(4):
            H[p] = L32[z_rows(p), mine_z] + dec(Zr[p])
        for k in (2, 1, 3):
            Hc[k - 1] = enc(H[(y + k) % 4])
            put(Hc.at[k - 1], Hr.at[k - 1], at_y(k), zw)

    def z_second():
        wait(zw)
        Ht[...] = enc(H[y] + dec(Hr[0]) + dec(Hr[1]) + dec(Hr[2]))
        here = lg.at[z_rows(y), mine_z]
        for k in (2, 1, 3):
            put(Ht, here, at_y(k), zy)
        put(Ht, here, across, zlast)
        kept.append(pltpu.make_async_copy(Ht, here, local.at[CHUNKS]))
        kept[-1].start()

    def z_third():
        wait(zy)
        for k in (1, 2, 3):
            there = lg.at[z_rows((y + k) % 4), mine_z]
            put(there, there, across, zlast)

    pz = []
    z_first()
    sum_l(0)
    sum_l(1)
    pz.append(sum_a(0))
    bs = sum_b()
    share_l(0)
    sum_l(2)
    pz.append(sum_a(1))
    z_second()
    share_l(1)
    share_l(2)
    z_third()

    wait(mates)
    mine = at_core(c)

    def total(view, first, second):
        a, b = first, second
        for k in range(3):
            a = a + dec(Pzr[k, view])
            b = b + dec(Bxr[k, view])
        return jnp.concatenate([a, b], axis=1)

    wait(pz[0])
    wait(pz[1])
    wait(bs)
    own = total(c, S32[zh, mine], B2[x, mine])
    other = total(o, So[...], Bo[...])
    first = c == 0
    ig[:, 0, :] = jnp.where(first, own, other)
    ig[:, 1, :] = jnp.where(first, other, own)

    wait(last)
    wait(zlast)
    for copy in kept:
        copy.wait()
    wait(sent)


def finish(ig, lg, image_grad, weight_grad, full, sem):
    copies = [pltpu.make_async_copy(ig, image_grad, sem.at[0])]
    copies[0].start()
    for j in range(5):
        at = pl.ds(j * 256, 256)
        full[at] = dec(lg[at])
        copies.append(pltpu.make_async_copy(full.at[at], weight_grad.at[at], sem.at[1 + j]))
        copies[-1].start()
    for copy in copies:
        copy.wait()


def shards(images, weight):
    V = pltpu.VMEM
    ig, lg = pl.pallas_call(
        kernel,
        out_shape=(
            jax.ShapeDtypeStruct((8, 2, D_IN), F32),
            jax.ShapeDtypeStruct((D_IN, BLOCK), BF16),
        ),
        in_specs=[pl.BlockSpec(memory_space=pltpu.HBM)] * 2,
        out_specs=[pl.BlockSpec(memory_space=V), pl.BlockSpec(memory_space=pl.ANY)],
        scratch_shapes=[
            V((8, 2, D_IN), BF16),
            V((D_IN, BLOCK), BF16),
            V((2, 8, D_IN), BF16),
            V((16, 16, D_IN), BF16),
            V((16, 16, D_IN), BF16),
            V((2, D_IN, M), BF16),
            V((D_IN, BLOCK), BF16),
            V((2 * BLOCK, D_IN), BF16),
            V((2, M, BLOCK), F32),
            V((M, 2 * BLOCK), BF16),
            V((M, BLOCK), BF16),
            V((3, M, BLOCK), F32),
            V((4, 32, 256), F32),
            V((4, 32, 256), BF16),
            V((3, 32, 256), BF16),
            V((32, 256), F32),
            V((32, 256), BF16),
            V((3, 32, 256), BF16),
            V((2, 4, 32, 256), BF16),
            V((8, 128), F32),
            V((3, 8, 128), F32),
            V((8, 128), F32),
            V((3, 8, 128), F32),
            V((2, 8, 128), F32),
            V((M, 2 * BLOCK), BF16),
            V((4, 4, 16, PCUT), F32),
            V((4, 4, 16, PCUT), BF16),
            V((3, 4, 16, PCUT), BF16),
            V((4, 16, PCUT), F32),
            V((4, 16, PCUT), BF16),
            V((3, 2, 8, PCUT), BF16),
            V((8, PCUT), F32),
            V((4, 4, 16, PREST), F32),
            V((4, 4, 16, PREST), BF16),
            V((3, 4, 16, PREST), BF16),
            V((4, 16, PREST), F32),
            V((4, 16, PREST), BF16),
            V((3, 2, 8, PREST), BF16),
            V((8, PREST), F32),
            V((D_IN, BLOCK), F32),
            V((3, LATE, BLOCK), BF16),
            V((3, LATE, BLOCK), BF16),
            V((LATE, BLOCK), BF16),
            V((LATE, BLOCK), BF16),
            V((LATE, BLOCK), BF16),
            V((4, ZROWS, 128), BF16),
            V((4, ZROWS, 128), BF16),
            V((4, ZROWS, 128), F32),
            V((3, ZROWS, 128), BF16),
            V((3, ZROWS, 128), BF16),
            V((ZROWS, 128), BF16),
            V((10240, 128), F32),
            pltpu.SemaphoreType.DMA,
            pltpu.SemaphoreType.DMA((NGROUPS,)),
            pltpu.SemaphoreType.DMA((CHUNKS + 1,)),
            pltpu.SemaphoreType.REGULAR,
        ],
        compiler_params=pltpu.CompilerParams(
            collective_id=0, has_side_effects=True, vmem_limit_bytes=VLIM
        ),
    )(pltpu.with_memory_space_constraint(images, pltpu.HBM), pltpu.with_memory_space_constraint(weight, pltpu.HBM))
    return pl.pallas_call(
        finish,
        out_shape=(
            jax.ShapeDtypeStruct((8, 2, D_IN), F32),
            jax.ShapeDtypeStruct((D_IN, BLOCK), F32),
        ),
        in_specs=[pl.BlockSpec(memory_space=V)] * 2,
        out_specs=[pl.BlockSpec(memory_space=pl.ANY)] * 2,
        scratch_shapes=[V((D_IN, BLOCK), F32), pltpu.SemaphoreType.DMA((6,))],
        compiler_params=pltpu.CompilerParams(vmem_limit_bytes=4 * 2**20),
    )(ig, lg)


NGROUPS = 30 + CHUNKS
VLIM = 24 * 2**20


def solution(mesh):
    return jax.shard_map(
        shards,
        mesh=mesh,
        in_specs=(P(("rep", "dp"), None, None), P(None, "dp")),
        out_specs=(P(("rep", "dp"), None, None), P(None, "dp")),
        check_vma=False,
    )
```

```python
import jax
import jax.numpy as jnp
from jax import lax
from jax.experimental import pallas as pl
from jax.experimental.pallas import tpu as pltpu
from jax.sharding import PartitionSpec as P

MESH = pl.DeviceIdType.MESH
F32, BF16 = jnp.float32, jnp.bfloat16

N_REP, N_DP = 8, 32
M = 256
D_IN = 1280
BLOCK = 256
EMB = BLOCK * N_DP
S = 8192.0 / N_REP
EPS = 0.0001
INV = S * 2.0 * 25.0 / (M * EMB)
VAR = S * 25.0 / (EMB * (M - 1))
COV = S * 4.0 / (EMB * (M - 1))
PIECE = D_IN // 4
SIZES = (64, 96, 96)
LATE = sum(SIZES)
ZROWS = PIECE - LATE
CHUNKS = len(SIZES)
CUT = 1024
REST = D_IN - CUT
PCUT = 1024
PREST = D_IN - PCUT
GRAM_UNIT = 2.0**-10


def root(t):
    return jnp.sqrt(jnp.abs(t))


def enc(v):
    return (v * jnp.abs(v)).astype(BF16)


def dec(b):
    t = b.astype(F32)
    s = root(t)
    return jnp.where(t < 0.0, -s, s)


def enc4(g):
    v = g * GRAM_UNIT
    return ((v * jnp.abs(v)) * (v * v)).astype(BF16)


def dec4(b):
    t = b.astype(F32)
    s = root(root(t)) * (1.0 / GRAM_UNIT)
    return jnp.where(t < 0.0, -s, s)


def nt(a, b):
    return lax.dot_general(a, b, (((1,), (1,)), ((), ())), preferred_element_type=F32)


def tn(a, b):
    return lax.dot_general(a, b, (((0,), (0,)), ((), ())), preferred_element_type=F32)


def nn(a, b):
    return jnp.dot(a, b, preferred_element_type=F32)


class Group:
    def __init__(self, sem):
        self.sem, self.kib = sem, 0


def kernel(
    img, w_hbm, ig, lg,
    Iv, w, I2, X, Xo, XT, Wo, WT, E, Cb, Cbo, base,
    T, Tc, Tx, Sz, Sc, Szr, TA, Dg, Dx, Ds, Dz, Dt,
    Ff,
    P32, Pc, Px, S32, Pz, Pzr, So,
    B32, Bc, Bz, B2, Bx, Bxr, Bo,
    L32, Ly, Lr, Lz, Lzr, La,
    Zc, Zr, H, Hc, Hr, Ht,
    span, send, recv, local, near,
):
    rep, dp = lax.axis_index("rep"), lax.axis_index("dp")
    y, zl = rep // 2, rep % 2
    c, chip = dp % 2, dp // 2
    x, zh = chip // 4, chip % 4
    o = 1 - c

    partner = (rep, chip * 2 + o)

    def at_x(k, core):
        return (rep, (((x + k) % 4) * 4 + zh) * 2 + core)

    def at_z(k, core):
        return (rep, (x * 4 + (zh + k) % 4) * 2 + core)

    def at_y(k):
        return (((y + k) % 4) * 2 + zl, dp)

    across = (y * 2 + (1 - zl), dp)

    fetch = pltpu.make_async_copy(img, Iv, local.at[0])
    fetch.start()
    wfetch = pltpu.make_async_copy(w_hbm, w, local.at[1])
    wfetch.start()
    barrier = pltpu.get_barrier_semaphore()
    peers = [at_z(k, core) for k in (1, 3) for core in (c, o)]
    for k in (2, 1, 3):
        peers += [at_x(k, c), at_x(k, o), at_y(k)]
    peers += [across, partner]
    for peer in peers:
        pl.semaphore_signal(barrier, inc=1, device_id=peer, device_id_type=MESH)
    fetch.wait()
    both = Iv[...].astype(F32)
    I2[0] = both[:, 0, :].astype(BF16)
    I2[1] = both[:, 1, :].astype(BF16)
    pl.semaphore_wait(barrier, len(peers))
    pl.semaphore_signal(near, inc=1, device_id=at_z(1, c), device_id_type=MESH)

    sent = Group(send)
    groups = []

    def group():
        groups.append(Group(recv.at[len(groups)]))
        return groups[-1]

    def put(src, dst, device, at=None):
        at = at or group()
        copy = pltpu.make_async_remote_copy(
            src_ref=src, dst_ref=dst, send_sem=sent.sem, recv_sem=at.sem,
            device_id=device, device_id_type=MESH,
        )
        copy.start()
        size = 1
        for n in src.shape:
            size *= n
        kib = size * jnp.dtype(src.dtype).itemsize // 1024
        at.kib += kib
        sent.kib += kib
        return at

    def wait(at):
        part = span.at[pl.ds(0, at.kib * 2)]
        pltpu.make_async_copy(part, part, at.sem).wait()

    at = pl.ds(pl.multiple_of(c * 8, 8), 8)
    A, B = pl.ds(0, CUT), pl.ds(CUT, REST)
    az, bx = {}, {}
    for k in (1, 3, 2):
        az[k], bx[k] = group(), group()
        for core in (c, o):
            if k != 2:
                put(I2.at[core, :, A], X.at[chip, at, A], at_z(k, core), az[k])
            put(I2.at[core, :, B], X.at[chip, at, B], at_x(k, core), bx[k])
    mate = put(I2.at[o], X.at[chip, at], partner)
    keep = pltpu.make_async_copy(I2.at[c], X.at[chip, at], local.at[0])
    keep.start()
    wswap = put(w_hbm, Wo, partner)
    keep.wait()
    wait(mate)
    forwards = group()
    for name, k in (("A", 0), ("A", 1), ("A", 3), ("B", 0), ("B", 1), ("B", 3), ("B", 2), ("A", 2)):
        if name == "A":
            if k:
                wait(az[k])
            slot = x * 4 + (zh - k + 4) % 4
            for j in (2, 1, 3):
                put(X.at[slot, :, A], X.at[slot, :, A], at_x(j, c), forwards)
            if k == 0:
                pl.semaphore_wait(near, 1)
                for core in (c, o):
                    put(I2.at[core, :, A], X.at[chip, at, A], at_z(2, core), az[2])
        else:
            if k:
                wait(bx[k])
            slot = ((x - k + 4) % 4) * 4 + zh
            for j in (2, 1, 3):
                put(X.at[slot, :, B], X.at[slot, :, B], at_z(j, c), forwards)
    wait(wswap)
    wfetch.wait()
    WT[0:BLOCK] = w[...].T
    WT[BLOCK:2 * BLOCK] = Wo[...].T
    wait(forwards)
    xswap = put(X, Xo, partner)

    rows = X[...].reshape(M, D_IN)
    for h, wr in enumerate((w, Wo)):
        e = nn(rows, wr[...])
        E[h] = e
        Cb[:, h * BLOCK:(h + 1) * BLOCK] = (e - jnp.mean(e, axis=0, keepdims=True)).astype(BF16)
    ri = lax.broadcasted_iota(jnp.int32, (128, 128), 0)
    ci = lax.broadcasted_iota(jnp.int32, (128, 128), 1)
    top = nt(Cb[0:128, :], Cb[...])
    low = nt(Cb[128:256, :], Cb[128:256, :])
    mixed = jnp.where(ri <= ci, top[:, 0:128], low)
    T[:, :, 0:128] = mixed.reshape(4, 32, 128)
    T[:, :, 128:256] = top[:, 128:256].reshape(4, 32, 128)
    Tc[...] = enc4(T[...])
    diags = [jnp.sum(jnp.where(ri == ci, g, 0.0), axis=0, keepdims=True) for g in (top[:, 0:128], low)]
    Dg[...] = jnp.where(lax.broadcasted_iota(jnp.int32, (8, 128), 0) == 0, diags[0], diags[1])
    ts = group()
    for k in (2, 1, 3):
        put(Tc.at[(x + k) % 4], Tx.at[k - 1], at_x(k, c), ts)
        put(Dg, Dx.at[k - 1], at_x(k, c), ts)
    wait(ts)
    s = T[x] + dec4(Tx[0]) + dec4(Tx[1]) + dec4(Tx[2])
    Sz[...] = s
    Sc[...] = enc4(s)
    Ds[...] = Dg[...] + Dx[0] + Dx[1] + Dx[2]
    ss = group()
    for k in (2, 1, 3):
        put(Sc, Szr.at[k - 1], at_z(k, c), ss)
        put(Ds, Dz.at[k - 1], at_z(k, c), ss)

    def ungrammed(e, gap, cb):
        centred = e - jnp.mean(e, axis=0, keepdims=True)
        spread = jnp.sqrt(jnp.sum(centred * centred, axis=0, keepdims=True) / (M - 1) + EPS)
        pull = jnp.where(spread < 1.0, -VAR / spread, 0.0)
        diag = jnp.sum(cb * cb, axis=0, keepdims=True) / (M - 1)
        return INV * gap + pull * centred - (COV * diag) * cb

    wait(xswap)
    orows = Xo[...].reshape(M, D_IN)
    for h, wr in enumerate((w, Wo)):
        e, eo = E[h], nn(orows, wr[...])
        cb = Cb[:, h * BLOCK:(h + 1) * BLOCK].astype(F32)
        base[h] = ungrammed(e, e - eo, cb)
        if h == 0:
            cb = (eo - jnp.mean(eo, axis=0, keepdims=True)).astype(BF16)
            Cbo[...] = cb
            base[2] = ungrammed(eo, eo - e, cb.astype(F32))
    XT[0] = rows.T
    XT[1] = orows.T

    wait(ss)
    TA[c, x] = enc4(Sz[...] + dec4(Szr[0]) + dec4(Szr[1]) + dec4(Szr[2]))
    gs, go = group(), group()
    for core, at in ((c, gs), (o, go)):
        for k in (2, 1, 3):
            put(TA.at[c, x], TA.at[c, x], at_x(k, core), at)
    put(TA.at[c, x], TA.at[c, x], partner, go)
    Dt[c] = Ds[...] + Dz[0] + Dz[1] + Dz[2]
    put(Dt.at[c], Dt.at[c], partner, go)
    wait(gs)
    def gram_of(view):
        mixed = dec4(TA[view, :, :, 0:128].reshape(128, 128))
        side = dec4(TA[view, :, :, 128:256].reshape(128, 128))
        flip = mixed.T
        ga = jnp.where(ri == ci, Dt[view, 0:1], jnp.where(ri < ci, mixed, flip))
        gd = jnp.where(ri == ci, Dt[view, 1:2], jnp.where(ri > ci, mixed, flip))
        gram = jnp.concatenate(
            [jnp.concatenate([ga, side], axis=1), jnp.concatenate([side.T, gd], axis=1)], axis=0
        )
        hi = gram.astype(BF16)
        return hi, (gram - hi.astype(F32)).astype(BF16)

    def feature_grad(gram, cb, rest):
        through = nn(gram[0], cb) + nn(gram[1], cb)
        return (rest + through * (COV / (M - 1))).astype(BF16)

    gram = gram_of(c)
    Ff[:, 0:BLOCK] = feature_grad(gram, Cb[:, 0:BLOCK], base[0])
    Ff[:, BLOCK:2 * BLOCK] = feature_grad(gram, Cb[:, BLOCK:2 * BLOCK], base[1])
    part = nn(Ff[...], WT[...])
    main = part[:, 0:PCUT].reshape(4, 4, 16, PCUT)
    P32[...] = main
    Pc[...] = enc(main)
    part = part[:, PCUT:D_IN].reshape(4, 4, 16, PREST)
    halves = (pl.ds(0, PCUT // 2), pl.ds(PCUT // 2, PCUT // 2))
    for j in range(4):
        B32[j] = part[:, j]
        Bc[j] = enc(part[:, j])
    L32[...] = nn(XT[0], Ff[:, 0:BLOCK])

    wait(go)
    L32[...] += nn(XT[1], feature_grad(gram_of(o), Cbo[...], base[2]))

    def chunk(q):
        return pl.ds(sum(SIZES[:q]), SIZES[q])

    def rows_of(k, q):
        return pl.ds(pl.multiple_of(((y + k) % 4) * PIECE + sum(SIZES[:q]), 16), SIZES[q])

    def z_rows(piece):
        return pl.ds(pl.multiple_of(piece * PIECE + LATE, 16), ZROWS)

    mine_z = pl.ds(pl.multiple_of(zl * 128, 128), 128)
    other_z = pl.ds(pl.multiple_of((1 - zl) * 128, 128), 128)
    for p in range(4):
        Zc[p] = enc(L32[z_rows(p), other_z])
    za = put(Zc, Zr, across)
    direct = {}
    for q in range(CHUNKS):
        direct[q] = group()
        for k in (2, 1, 3):
            Ly[k - 1, chunk(q)] = enc(L32[rows_of(k, q)])
            put(Ly.at[k - 1, chunk(q)], Lr.at[k - 1, chunk(q)], at_y(k), direct[q])
    ps = [group(), group()]
    bz = group()
    for i in range(2):
        for k in (2, 1, 3):
            put(Pc.at[(x + k) % 4, :, :, halves[i]], Px.at[k - 1, :, :, halves[i]], at_x(k, c), ps[i])
        if i == 0:
            for k in (2, 1, 3):
                put(Bc.at[(zh + k) % 4], Bz.at[k - 1], at_z(k, c), bz)
    def at_core(core):
        return pl.ds(pl.multiple_of(core * 8, 8), 8)

    mates = group()

    def sum_a(i):
        wait(ps[i])
        cols = halves[i]
        for j in range(4):
            s = P32[x, j, :, cols] + dec(Px[0, j, :, cols]) + dec(Px[1, j, :, cols]) + dec(Px[2, j, :, cols])
            S32[j, :, cols] = s
            Pz[j, :, cols] = enc(s)
        at = group()
        for k in (2, 1, 3):
            for core in (c, o):
                put(Pz.at[(zh + k) % 4, at_core(core), cols], Pzr.at[k - 1, c, :, cols], at_z(k, core), at)
        put(S32.at[zh, at_core(o), cols], So.at[:, cols], partner, mates)
        return at

    def sum_b():
        wait(bz)
        for j in range(4):
            s = B32[zh, j] + dec(Bz[0, j]) + dec(Bz[1, j]) + dec(Bz[2, j])
            B2[j] = s
            Bx[j] = enc(s)
        at = group()
        for k in (2, 1, 3):
            for core in (c, o):
                put(Bx.at[(x + k) % 4, at_core(core)], Bxr.at[k - 1, c], at_x(k, core), at)
        put(B2.at[x, at_core(o)], Bo, partner, mates)
        return at

    zz, kept = {}, []
    last = group()

    def sum_l(q):
        wait(direct[q])
        at = chunk(q)
        Lz[at] = enc(L32[rows_of(0, q)] + dec(Lr[0, at]) + dec(Lr[1, at]) + dec(Lr[2, at]))
        zz[q] = put(Lz.at[at], Lzr.at[at], across)

    def share_l(q):
        wait(zz[q])
        at = chunk(q)
        La[at] = enc(dec(Lz[at]) + dec(Lzr[at]))
        here = lg.at[rows_of(0, q)]
        for k in (2, 1, 3):
            put(La.at[at], here, at_y(k), last)
        kept.append(pltpu.make_async_copy(La.at[at], here, local.at[q]))
        kept[-1].start()

    zw = group()
    zy = group()
    zlast = group()

    def z_first():
        wait(za)
        for p in range(4):
            H[p] = L32[z_rows(p), mine_z] + dec(Zr[p])
        for k in (2, 1, 3):
            Hc[k - 1] = enc(H[(y + k) % 4])
            put(Hc.at[k - 1], Hr.at[k - 1], at_y(k), zw)

    def z_second():
        wait(zw)
        Ht[...] = enc(H[y] + dec(Hr[0]) + dec(Hr[1]) + dec(Hr[2]))
        here = lg.at[z_rows(y), mine_z]
        for k in (2, 1, 3):
            put(Ht, here, at_y(k), zy)
        put(Ht, here, across, zlast)
        kept.append(pltpu.make_async_copy(Ht, here, local.at[CHUNKS]))
        kept[-1].start()

    def z_third():
        wait(zy)
        for k in (1, 2, 3):
            there = lg.at[z_rows((y + k) % 4), mine_z]
            put(there, there, across, zlast)

    pz = []
    z_first()
    sum_l(0)
    sum_l(1)
    pz.append(sum_a(0))
    bs = sum_b()
    share_l(0)
    sum_l(2)
    pz.append(sum_a(1))
    z_second()
    share_l(1)
    share_l(2)
    z_third()

    wait(mates)
    mine = at_core(c)

    def total(view, first, second):
        a, b = first, second
        for k in range(3):
            a = a + dec(Pzr[k, view])
            b = b + dec(Bxr[k, view])
        return jnp.concatenate([a, b], axis=1)

    wait(pz[0])
    wait(pz[1])
    wait(bs)
    own = total(c, S32[zh, mine], B2[x, mine])
    other = total(o, So[...], Bo[...])
    first = c == 0
    ig[:, 0, :] = jnp.where(first, own, other)
    ig[:, 1, :] = jnp.where(first, other, own)

    wait(last)
    wait(zlast)
    for copy in kept:
        copy.wait()
    wait(sent)


def finish(ig, lg, image_grad, weight_grad, full, sem):
    copies = [pltpu.make_async_copy(ig, image_grad, sem.at[0])]
    copies[0].start()
    for j in range(5):
        at = pl.ds(j * 256, 256)
        full[at] = dec(lg[at])
        copies.append(pltpu.make_async_copy(full.at[at], weight_grad.at[at], sem.at[1 + j]))
        copies[-1].start()
    for copy in copies:
        copy.wait()


def shards(images, weight):
    V = pltpu.VMEM
    ig, lg = pl.pallas_call(
        kernel,
        out_shape=(
            jax.ShapeDtypeStruct((8, 2, D_IN), F32),
            jax.ShapeDtypeStruct((D_IN, BLOCK), BF16),
        ),
        in_specs=[pl.BlockSpec(memory_space=pltpu.HBM)] * 2,
        out_specs=[pl.BlockSpec(memory_space=V), pl.BlockSpec(memory_space=pl.ANY)],
        scratch_shapes=[
            V((8, 2, D_IN), BF16),
            V((D_IN, BLOCK), BF16),
            V((2, 8, D_IN), BF16),
            V((16, 16, D_IN), BF16),
            V((16, 16, D_IN), BF16),
            V((2, D_IN, M), BF16),
            V((D_IN, BLOCK), BF16),
            V((2 * BLOCK, D_IN), BF16),
            V((2, M, BLOCK), F32),
            V((M, 2 * BLOCK), BF16),
            V((M, BLOCK), BF16),
            V((3, M, BLOCK), F32),
            V((4, 32, 256), F32),
            V((4, 32, 256), BF16),
            V((3, 32, 256), BF16),
            V((32, 256), F32),
            V((32, 256), BF16),
            V((3, 32, 256), BF16),
            V((2, 4, 32, 256), BF16),
            V((8, 128), F32),
            V((3, 8, 128), F32),
            V((8, 128), F32),
            V((3, 8, 128), F32),
            V((2, 8, 128), F32),
            V((M, 2 * BLOCK), BF16),
            V((4, 4, 16, PCUT), F32),
            V((4, 4, 16, PCUT), BF16),
            V((3, 4, 16, PCUT), BF16),
            V((4, 16, PCUT), F32),
            V((4, 16, PCUT), BF16),
            V((3, 2, 8, PCUT), BF16),
            V((8, PCUT), F32),
            V((4, 4, 16, PREST), F32),
            V((4, 4, 16, PREST), BF16),
            V((3, 4, 16, PREST), BF16),
            V((4, 16, PREST), F32),
            V((4, 16, PREST), BF16),
            V((3, 2, 8, PREST), BF16),
            V((8, PREST), F32),
            V((D_IN, BLOCK), F32),
            V((3, LATE, BLOCK), BF16),
            V((3, LATE, BLOCK), BF16),
            V((LATE, BLOCK), BF16),
            V((LATE, BLOCK), BF16),
            V((LATE, BLOCK), BF16),
            V((4, ZROWS, 128), BF16),
            V((4, ZROWS, 128), BF16),
            V((4, ZROWS, 128), F32),
            V((3, ZROWS, 128), BF16),
            V((3, ZROWS, 128), BF16),
            V((ZROWS, 128), BF16),
            V((10240, 128), F32),
            pltpu.SemaphoreType.DMA,
            pltpu.SemaphoreType.DMA((NGROUPS,)),
            pltpu.SemaphoreType.DMA((CHUNKS + 1,)),
            pltpu.SemaphoreType.REGULAR,
        ],
        compiler_params=pltpu.CompilerParams(
            collective_id=0, has_side_effects=True, vmem_limit_bytes=VLIM
        ),
    )(pltpu.with_memory_space_constraint(images, pltpu.HBM), pltpu.with_memory_space_constraint(weight, pltpu.HBM))
    return pl.pallas_call(
        finish,
        out_shape=(
            jax.ShapeDtypeStruct((8, 2, D_IN), F32),
            jax.ShapeDtypeStruct((D_IN, BLOCK), F32),
        ),
        in_specs=[pl.BlockSpec(memory_space=V)] * 2,
        out_specs=[pl.BlockSpec(memory_space=pl.ANY)] * 2,
        scratch_shapes=[V((D_IN, BLOCK), F32), pltpu.SemaphoreType.DMA((6,))],
        compiler_params=pltpu.CompilerParams(vmem_limit_bytes=4 * 2**20),
    )(ig, lg)


NGROUPS = 30 + CHUNKS
VLIM = 24 * 2**20


def solution(mesh):
    return jax.shard_map(
        shards,
        mesh=mesh,
        in_specs=(P(("rep", "dp"), None, None), P(None, "dp")),
        out_specs=(P(("rep", "dp"), None, None), P(None, "dp")),
        check_vma=False,
    )
```
